256 devices in a mesh: term: 8 (over z), sec: 32 (over y, x, core).
Axes of the slice: x: 4, y: 4, z: 8, core: 2. Of those that a mesh axis runs over, the one named last changes fastest.
Arguments:
- start_vectors: bfloat16 [2, 64, 256, 256], P(None, 'sec'), may hold values from -6 to 6
- left_env: bfloat16 [32, 64, 256, 256], P('term', 'sec'), may hold values from -0.375 to 0.375
- right_env: bfloat16 [32, 64, 256, 256], P('term', 'sec'), may hold values from -0.375 to 0.375
- term_shift: int32 [32], P('term'), may hold values from -1 to 1
- precond: float32 [64, 256, 256], P('sec'), may hold values from 0.25 to 4
- block_dims: int32 [64], P('sec'), may hold values from 1 to 256, 8192 in all
Outputs:
- vector: float32 [2, 64, 256, 256], P(None, 'sec', 'term')
- energy: float32 [2], replicated
The draws below stay inside these ranges and needn't reach their ends.
Inputs may be any that keep to these rules, and one draw needn't show every extreme that they name: `block_dims`: one block has exactly 256 live states.
All inputs are finite; a program needn't handle non-finite values.
Results may differ from the reference program's by a relative error of at most 0.0036.
Values may be sent and summed in bfloat16 or wider, within the bound.
No kernel may reach another device: no remote copies, remote signals or barrier semaphores. Data moves between devices by JAX's collectives and lax.ppermute only.
A program may use at most 64 MiB of HBM per device.

```python
import math
import jax
import jax.numpy as jnp
import numpy as np
from jax import lax

M = 256
NV = 2
ITERS = 2
NB = 64
K = 32


def set_ends(array, rng, smallest, high):
    place = [jax.random.randint(jax.random.fold_in(rng, axis), (), 0, length) for axis, length in enumerate(array.shape)]
    longest = array.shape.index(max(array.shape))
    next_to = place[:longest] + [(place[longest] + 1) % array.shape[longest]] + place[longest + 1:]
    return array.at[tuple(place)].set(smallest).at[tuple(next_to)].set(high)


def level_of(key, shape, shards, low, top_value):
    def one(axis_at, shards_of):
        steps = jax.random.uniform(jax.random.fold_in(jax.random.fold_in(key, 6), axis_at), (shards_of,), jnp.float32, low / len(shards), top_value / len(shards))
        return jnp.repeat(jnp.exp(steps), shape[axis_at] // shards_of).reshape((-1,) + (1,) * (len(shape) - axis_at - 1))

    gain = one(*shards[0])
    for cut in shards[1:]:
        gain = gain * one(*cut)
    return gain


def split_up(amount, total, reach, lean):
    loads = [(1 << 20) // math.isqrt(rank ** lean) + 1 for rank in range(2, amount + 1)]
    spare, given = total - reach - (amount - 1), [1] * (amount - 1)
    while spare > 0:
        movable = [i for i in range(amount - 1) if given[i] < reach]
        pool, budget = sum([loads[i] for i in movable]), spare
        for i in movable:
            more = min(reach - given[i], max(1, budget * loads[i] // pool), spare)
            given[i] = given[i] + more
            spare = spare - more
    return np.array([reach] + given)


def uneven(rng, number_of, total, reach, skew):
    if number_of == 2:
        one = jax.random.randint(rng, (), max(1, total - reach), min(reach, total - 1) + 1)
        return jnp.stack([one, total - one])
    tallies = jnp.asarray(split_up(number_of, total, reach, skew), jnp.int32)
    twos = (number_of - 1) // 2
    giver, receiver = tallies[1:1 + 2 * twos:2], tallies[2:2 + 2 * twos:2]
    room = jnp.minimum(giver - 1, reach - receiver)
    moved = jax.random.randint(jax.random.fold_in(rng, 1), (twos,), 0, 1 << 20) % (room + 1)
    tallies = tallies.at[1:1 + 2 * twos:2].set(giver - moved).at[2:2 + 2 * twos:2].set(receiver + moved)
    return tallies[jax.random.permutation(jax.random.fold_in(rng, 2), number_of)]


def normal_values(own_key, shape, deviation, most, split=(), held_as=jnp.bfloat16):
    entries = jax.random.normal(own_key, shape, jnp.float32) * deviation
    if len(split) > 0:
        entries = level_of(own_key, shape, split, -0.22, 0.18) * entries
    return jnp.clip(entries, min=-most, max=most).astype(held_as)


def setup_inputs(seed: int = 0) -> dict:
    arg_keys = jax.random.split(jax.random.key(seed), 7)
    start_vectors = normal_values(arg_keys[0], (NV, NB, M, M), 1.0, 6.0, ((1, 32),))
    left_env = normal_values(arg_keys[1], (K, NB, M, M), M ** -0.5, 0.375, ((0, 8), (1, 32)))
    right_env = normal_values(arg_keys[2], (K, NB, M, M), M ** -0.5, 0.375, ((0, 8), (1, 32)))
    term_shift = set_ends(jax.random.randint(arg_keys[3], (K,), -1, 2), jax.random.fold_in(arg_keys[3], 1), -1, 1).astype(jnp.int32)
    precond = jnp.clip(jnp.exp(math.log(4.0) - 2.7725887 * jax.random.uniform(arg_keys[4], (NB, M, M), jnp.float32) ** level_of(arg_keys[4], (NB, M, M), ((0, 32),), -0.2, 0.2)), 0.25, 4.0)
    block_dims = uneven(arg_keys[5], NB, NB * M // 2, M, 1).astype(jnp.int32)
    return {"start_vectors": start_vectors, "left_env": left_env, "right_env": right_env, "term_shift": term_shift, "precond": precond, "block_dims": block_dims}


def block_mask(block_dims):
    position = jnp.arange(M, dtype=jnp.int32)
    live_rows = position[None, :, None] < block_dims[:, None, None]
    live_cols = position[None, None, :] < block_dims[:, None, None]
    return (live_rows & live_cols).astype(jnp.float32)

def apply_op(vector_bf, left_env, right_env, term_shift, mask):
    vector_wide = vector_bf.astype(jnp.float32)

    def one_term(total, packed):
        left_one, right_one, offset = packed
        product = jnp.einsum('ujab,jcb->ujac', vector_wide, right_one.astype(jnp.float32)).astype(jnp.bfloat16)
        padded = jnp.pad(product, ((0, 0), (1, 1), (0, 0), (0, 0)))
        chosen = lax.dynamic_slice_in_dim(padded, (offset + 1).astype(jnp.int32), NB, axis=1)
        total = total + jnp.einsum('bac,ubcd->ubad', left_one.astype(jnp.float32), chosen.astype(jnp.float32))
        return (total, None)
    initial = jnp.zeros((NV, NB, M, M), jnp.float32)
    total, _ = lax.scan(one_term, initial, (left_env, right_env, term_shift))
    return total * mask

def reference(start_vectors, left_env, right_env, term_shift, precond, block_dims):
    mask = block_mask(block_dims)
    factor = 1.0 / (NB * M * M)

    def inner(left, right):
        return lax.optimization_barrier(jnp.sum(left * right, axis=(1, 2, 3))) * factor

    def expand(value):
        return value[:, None, None, None]
    start = start_vectors * mask.astype(jnp.bfloat16)
    h_vec = apply_op(start, left_env, right_env, term_shift, mask)
    vector = start.astype(jnp.float32)
    length = jnp.sqrt(inner(vector, vector) + 1e-06)
    vector = vector / expand(length)
    h_vec = h_vec / expand(length)
    energy = jnp.zeros((NV,), jnp.float32)
    for iteration in range(ITERS):
        rayleigh = inner(vector, h_vec)
        resid = h_vec - expand(rayleigh) * vector
        precon_res = precond[None] * resid
        correlation = inner(vector, precon_res)
        direction = precon_res - expand(correlation) * vector
        dir_norm = jnp.sqrt(inner(direction, direction) + 1e-06)
        coupling = inner(direction, h_vec) / dir_norm
        direction = direction / expand(dir_norm)
        h_dir = apply_op(direction.astype(jnp.bfloat16), left_env, right_env, term_shift, mask)
        curvature = inner(direction, h_dir)
        energy = 0.5 * (rayleigh + curvature) - jnp.sqrt((0.5 * (rayleigh - curvature)) ** 2 + coupling ** 2)
        weight = energy - rayleigh
        new_size = jnp.sqrt(coupling ** 2 + weight ** 2)
        vector = (expand(coupling) * vector + expand(weight) * direction) / expand(new_size)
        h_vec = (expand(coupling) * h_vec + expand(weight) * h_dir) / expand(new_size)
    return (vector, energy)
```

```python
import jax
import jax.numpy as jnp
from jax import lax
from jax.experimental import pallas as pl
from jax.experimental.pallas import tpu as pltpu
from jax.sharding import PartitionSpec as P

BF = jnp.bfloat16
F32 = jnp.float32


def apply_kernel(slot_ref, x_ref, right_ref, left_ref, out_ref):
    vecs, _, states, _ = x_ref.shape
    terms, blocks = left_ref.shape[:2]
    groups, share = out_ref.shape[0], out_ref.shape[3]
    for b in range(blocks):
        acc = jnp.zeros((states, vecs * states), F32)
        for k in range(terms):
            slot = slot_ref[k, b]
            x = x_ref[:, slot].reshape(vecs * states, states)
            z = lax.dot_general(
                x, right_ref[k, slot], (((1,), (1,)), ((), ())), preferred_element_type=F32
            ).astype(BF)
            wide = jnp.concatenate([z[u * states : (u + 1) * states] for u in range(vecs)], axis=1)
            acc = acc + jnp.dot(left_ref[k, b], wide, preferred_element_type=F32)
        for u in range(vecs):
            part = acc[:, u * states : (u + 1) * states]
            out_ref[:, u, b] = part.reshape(groups, share, states).astype(out_ref.dtype)


def shards(start_vectors, left_env, right_env, term_shift, precond, block_dims):
    vecs, blocks, states, _ = start_vectors.shape
    groups = lax.axis_size("term")
    sec = lax.axis_size("sec")
    share = states // groups
    core = lax.axis_index("sec") % 2
    term = lax.axis_index("term")
    factor = 1.0 / (blocks * sec * states * states)
    position = jnp.arange(states, dtype=jnp.int32)
    live_rows = position[None, :, None] < block_dims[:, None, None]
    live_cols = position[None, None, :] < block_dims[:, None, None]
    mask = (live_rows & live_cols).astype(F32)

    core_pairs = [(i, i ^ 1) for i in range(sec)]
    chip_pairs = [(i, i + 1) for i in range(1, sec - 1, 2)]
    chip_pairs = chip_pairs + [(j, i) for i, j in chip_pairs]
    same_core = [[2 * c + k for c in range(sec // 2)] for k in range(2)]

    def edges(x, axis):
        inner = lax.dynamic_index_in_dim(x, 1 - core, axis, keepdims=True)
        outer = lax.dynamic_index_in_dim(x, core, axis, keepdims=True)
        return lax.ppermute(inner, "sec", core_pairs), lax.ppermute(outer, "sec", chip_pairs)

    def with_edges(x, axis):
        return jnp.concatenate([x, *edges(x, axis)], axis=axis)

    def rows(x, axis):
        return lax.dynamic_slice_in_dim(x, term * share, share, axis)

    at = jnp.arange(blocks, dtype=jnp.int32)[None, :] + term_shift[:, None]
    slot = jnp.where(at < 0, 3 - core, jnp.where(at > 1, 2 + core, at)).astype(jnp.int32)

    apply_op = pl.pallas_call(
        apply_kernel,
        out_shape=jax.ShapeDtypeStruct((groups, vecs, blocks, share, states), BF),
        in_specs=[pl.BlockSpec(memory_space=pltpu.SMEM)]
        + [pl.BlockSpec(memory_space=pltpu.VMEM)] * 3,
        out_specs=pl.BlockSpec(memory_space=pltpu.VMEM),
        cost_estimate=pl.CostEstimate(
            flops=8 * vecs * blocks * states**3 * 2, bytes_accessed=5 << 20, transcendentals=0
        ),
    )

    def scatter_sum(parts):
        got = lax.all_to_all(parts, "term", 0, 0)
        return jnp.sum(got.astype(F32), axis=0) * mask_rows

    def pieces(values):
        high = lax.reduce_precision(values, 8, 7)
        rest = values - high
        middle = lax.reduce_precision(rest, 8, 7)
        low = lax.reduce_precision(rest - middle, 8, 7)
        return jnp.concatenate([high, middle, low])

    def gather(part, scalars):
        count = scalars.size
        packed = jnp.pad(pieces(scalars.reshape(-1)), (0, 16 * states - 3 * count))
        body = jnp.concatenate(
            [part.reshape(-1, states).astype(BF), packed.reshape(16, states).astype(BF)]
        )
        got = lax.all_to_all(jnp.broadcast_to(body[None], (groups,) + body.shape), "term", 0, 0)
        main = got[:, :-16].reshape(groups, vecs, blocks, share, states)
        main = main.transpose(1, 2, 0, 3, 4).reshape(vecs, blocks, states, states)
        small = got[:, -16:].reshape(groups, 16 * states)[:, : 3 * count].astype(F32)
        small = jnp.sum(small.reshape(groups, 3, count), axis=(0, 1))
        return main, small

    def sum_sec(values):
        count = values.size
        row = jnp.pad(values, (0, 128 - count))[None]
        row = row + lax.ppermute(row, "sec", core_pairs)
        got = lax.all_to_all(
            jnp.broadcast_to(row[None], (sec // 2,) + row.shape),
            "sec",
            0,
            0,
            axis_index_groups=same_core,
        )
        return jnp.sum(got, axis=0)[0, :count]

    def dots(left, right):
        return jnp.sum(left * right, axis=(1, 2, 3)) * factor

    def expand(value):
        return value[:, None, None, None]

    start = start_vectors * mask.astype(BF)
    right_all = with_edges(right_env, 1)
    start_all = with_edges(start, 1)
    pre_all = with_edges(precond, 0)
    mask_rows = rows(mask, 1)
    pre = rows(precond, 1)[None]
    vec = rows(start, 2).astype(F32)

    h_raw = scatter_sum(apply_op(slot, start_all, right_all, left_env))
    mv, mh = pre * vec, pre * h_raw
    gram = jnp.stack(
        [
            dots(vec, vec),
            dots(vec, h_raw),
            dots(vec, mv),
            dots(vec, mh),
            dots(h_raw, mh),
            dots(mv, mv),
            dots(mv, mh),
            dots(mh, mh),
        ]
    )
    h_all, small = gather(h_raw, gram)
    h_all = with_edges(h_all, 1)
    total = sum_sec(small).reshape(8, vecs)
    scale = 1.0 / jnp.sqrt(total[0] + 1e-06)
    vv, vh, vmv, vmh, hmh, mvmv, mvmh, mhmh = total * scale**2
    correlation = vmh - vh * vmv
    square = (
        mhmh
        - 2.0 * vh * mvmh
        + vh**2 * mvmv
        - 2.0 * correlation * (vmh - vh * vmv)
        + correlation**2 * vv
    )
    dir_norm = jnp.sqrt(jnp.maximum(square, 0.0) + 1e-06)
    coupling = (hmh - vh * vmh - correlation * vh) / dir_norm
    rayleigh = vh

    def direct(v, h, m):
        raw = m * (h - expand(rayleigh) * v) - expand(correlation) * v
        return raw * expand(scale / dir_norm)

    dir_all = direct(start_all.astype(F32), h_all.astype(F32), pre_all[None])
    direction = direct(vec, h_raw, pre)
    vec = vec * expand(scale)
    h_vec = h_raw * expand(scale)
    h_dir = scatter_sum(apply_op(slot, dir_all.astype(BF), right_all, left_env))

    basis = [vec, direction, h_vec, h_dir]
    weighted = [pre * x for x in basis]
    pairs = [(i, j) for i in range(4) for j in range(i, 4)]
    plain = [(0, 0), (0, 1), (1, 1), (0, 2), (0, 3), (1, 2), (1, 3)]
    gram = jnp.stack(
        [dots(basis[i], basis[j]) for i, j in plain]
        + [dots(basis[i], weighted[j]) for i, j in pairs]
        + [dots(weighted[i], weighted[j]) for i, j in pairs]
    )
    hd_all, small = gather(h_dir, gram)
    hd_all = with_edges(hd_all, 1)
    total = sum_sec(small).reshape(-1, vecs)
    one = {p: total[i] for i, p in enumerate(plain)}
    first = {p: total[len(plain) + i] for i, p in enumerate(pairs)}
    second = {p: total[len(plain) + len(pairs) + i] for i, p in enumerate(pairs)}

    def form(table, left, right):
        result = 0.0
        for i, x in left:
            for j, y in right:
                result = result + x * y * table[(min(i, j), max(i, j))]
        return result

    curvature = one[(1, 3)]
    energy = 0.5 * (rayleigh + curvature) - jnp.sqrt(
        (0.5 * (rayleigh - curvature)) ** 2 + coupling**2
    )
    weight = energy - rayleigh
    size = jnp.sqrt(coupling**2 + weight**2)
    keep, mix = coupling / size, weight / size
    v_of, h_of = [(0, keep), (1, mix)], [(2, keep), (3, mix)]
    rayleigh = form(one, v_of, h_of)
    resid_of = h_of + [(i, -rayleigh * x) for i, x in v_of]
    correlation = form(first, v_of, resid_of)
    square = (
        form(second, resid_of, resid_of)
        - 2.0 * correlation * form(first, v_of, resid_of)
        + correlation**2 * form(one, v_of, v_of)
    )
    dir_norm = jnp.sqrt(jnp.maximum(square, 0.0) + 1e-06)
    coupling = (form(first, resid_of, h_of) - correlation * rayleigh) / dir_norm

    def advance(v, d, h, hd, m):
        new_v = expand(keep) * v + expand(mix) * d
        new_h = expand(keep) * h + expand(mix) * hd
        raw = m * (new_h - expand(rayleigh) * new_v) - expand(correlation) * new_v
        return new_v, raw / expand(dir_norm)

    _, dir_all = advance(
        start_all.astype(F32) * expand(scale),
        dir_all,
        h_all.astype(F32) * expand(scale),
        hd_all.astype(F32),
        pre_all[None],
    )
    vec, direction = advance(vec, direction, h_vec, h_dir, pre)
    parts = apply_op(slot, dir_all.astype(BF), right_all, left_env)
    own = dir_all[:, :blocks].reshape(vecs, blocks, groups, share, states).transpose(2, 0, 1, 3, 4)
    curvature = jnp.sum(parts.astype(F32) * own, axis=(0, 2, 3, 4)) * factor
    row = jnp.pad(curvature, (0, 128 - vecs))[None]
    everyone = groups * sec
    got = lax.all_to_all(
        jnp.broadcast_to(row[None], (everyone,) + row.shape), ("term", "sec"), 0, 0
    )
    curvature = jnp.sum(got, axis=0)[0, :vecs]
    energy = 0.5 * (rayleigh + curvature) - jnp.sqrt(
        (0.5 * (rayleigh - curvature)) ** 2 + coupling**2
    )
    weight = energy - rayleigh
    size = jnp.sqrt(coupling**2 + weight**2)
    final = (expand(coupling) * vec + expand(weight) * direction) / expand(size)
    return (final, energy)


def solution(mesh):
    return jax.shard_map(
        shards,
        mesh=mesh,
        in_specs=(
            P(None, "sec", None, None),
            P("term", "sec", None, None),
            P("term", "sec", None, None),
            P("term"),
            P("sec", None, None),
            P("sec"),
        ),
        out_specs=(P(None, "sec", "term", None), P()),
        check_vma=False,
    )
```

```python
import functools

import jax
import jax.numpy as jnp
from jax import lax
from jax.experimental import pallas as pl
from jax.experimental.pallas import tpu as pltpu
from jax.sharding import PartitionSpec as P

BF = jnp.bfloat16
F32 = jnp.float32


def apply_kernel(count, slot_ref, x_ref, right_ref, left_ref, *refs):
    field_refs, paired_refs, rest = refs[: count[0]], refs[count[0] : sum(count)], refs[sum(count) :]
    out_ref, z_ref = rest[0], rest[-1]
    vecs, _, states, _ = x_ref.shape
    terms, blocks = left_ref.shape[:2]
    for k in range(terms):
        for b in range(blocks):
            slot = slot_ref[k, b]
            x = x_ref[:, slot].reshape(vecs * states, states)
            z = lax.dot_general(
                x, right_ref[k, slot], (((1,), (1,)), ((), ())), preferred_element_type=F32
            ).astype(BF)
            for u in range(vecs):
                z_ref[b, pl.ds(k * states, states), pl.ds(u * states, states)] = z[
                    u * states : (u + 1) * states
                ]
    if sum(count):
        dot_ref = rest[-2]
        dot_ref[...] = jnp.zeros_like(dot_ref)
    for b in range(blocks):
        wide = jnp.concatenate([left_ref[k, b] for k in range(terms)], axis=1)
        acc = jnp.dot(wide, z_ref[b], preferred_element_type=F32)
        for u in range(vecs):
            part = acc[:, u * states : (u + 1) * states]
            if not sum(count):
                groups, share = out_ref.shape[0], out_ref.shape[3]
                out_ref[:, u, b] = part.reshape(groups, share, states).astype(out_ref.dtype)
            elif len(rest) == 3:
                out_ref[u, b] = part.astype(out_ref.dtype)
            products = [part * f[u, b].astype(F32) for f in field_refs]
            products += [x_ref[u, b].astype(F32) * f[u, b].astype(F32) for f in paired_refs]
            for i, product in enumerate(products):
                folded = jnp.sum(product.reshape(states // 8, 8, states), axis=0)
                dot_ref[i, u] = dot_ref[i, u] + folded[:, :128] + folded[:, 128:]


def shards(start_vectors, left_env, right_env, term_shift, precond, block_dims):
    vecs, blocks, states, _ = start_vectors.shape
    groups = lax.axis_size("term")
    sec = lax.axis_size("sec")
    share = states // groups
    core = lax.axis_index("sec") % 2
    term = lax.axis_index("term")
    factor = 1.0 / (blocks * sec * states * states)
    position = jnp.arange(states, dtype=jnp.int32)
    live_rows = position[None, :, None] < block_dims[:, None, None]
    live_cols = position[None, None, :] < block_dims[:, None, None]
    mask = (live_rows & live_cols).astype(F32)

    core_pairs = [(i, i ^ 1) for i in range(sec)]
    chip_pairs = [(i, i + 1) for i in range(1, sec - 1, 2)]
    chip_pairs = chip_pairs + [(j, i) for i, j in chip_pairs]

    def edges(x, axis):
        inner = lax.dynamic_index_in_dim(x, 1 - core, axis, keepdims=True)
        outer = lax.dynamic_index_in_dim(x, core, axis, keepdims=True)
        return lax.ppermute(inner, "sec", core_pairs), lax.ppermute(outer, "sec", chip_pairs)

    def with_edges(x, axis):
        return jnp.concatenate([x, *edges(x, axis)], axis=axis)

    def rows(x, axis):
        return lax.dynamic_slice_in_dim(x, term * share, share, axis)

    at = jnp.arange(blocks, dtype=jnp.int32)[None, :] + term_shift[:, None]
    slot = jnp.where(at < 0, 3 - core, jnp.where(at > 1, 2 + core, at)).astype(jnp.int32)

    def apply_op(x, fields=(), paired=(), keep=True):
        outs = []
        if not fields:
            outs = [jax.ShapeDtypeStruct((groups, vecs, blocks, share, states), BF)]
        elif keep:
            outs = [jax.ShapeDtypeStruct((vecs, blocks, states, states), BF)]
        count = (len(fields), len(paired))
        if sum(count):
            outs.append(jax.ShapeDtypeStruct((sum(count), vecs, 8, 128), F32))
        vmem = pl.BlockSpec(memory_space=pltpu.VMEM)
        result = pl.pallas_call(
            functools.partial(apply_kernel, count),
            out_shape=outs,
            in_specs=[pl.BlockSpec(memory_space=pltpu.SMEM)] + [vmem] * (3 + sum(count)),
            out_specs=[vmem] * len(outs),
            scratch_shapes=[pltpu.VMEM((blocks, left_env.shape[0] * states, vecs * states), BF)],
            compiler_params=pltpu.CompilerParams(vmem_limit_bytes=24 << 20),
            cost_estimate=pl.CostEstimate(
                flops=16 * vecs * blocks * states**3, bytes_accessed=5 << 20, transcendentals=0
            ),
        )(slot, x, right_all, left_env, *fields, *paired)
        return result[0] if len(outs) == 1 else result

    def exchange(parts):
        return lax.all_to_all(parts, "term", 0, 0)

    def settle(got):
        return jnp.sum(got.astype(F32), axis=0) * mask_rows

    def gather(part):
        body = part.astype(BF)
        got = exchange(jnp.broadcast_to(body[None], (groups,) + body.shape))
        return got.transpose(1, 2, 0, 3, 4).reshape(vecs, blocks, states, states)

    def sum_all(values):
        count = values.size
        row = jnp.pad(values.reshape(-1), (0, 128 - count))[None]
        everyone = groups * sec
        got = lax.all_to_all(
            jnp.broadcast_to(row[None], (everyone,) + row.shape), ("term", "sec"), 0, 0
        )
        return jnp.sum(got, axis=0)[0, :count].reshape(values.shape)

    def dots(left, right):
        return jnp.sum(left * right, axis=(1, 2, 3)) * factor

    def expand(value):
        return value[:, None, None, None]

    start = start_vectors * mask.astype(BF)
    right_all = with_edges(right_env, 1)
    start_all = with_edges(start, 1)
    mask_rows = rows(mask, 1)
    pre = rows(precond, 1)[None]
    vec = rows(start, 2).astype(F32)

    parts, pre_late = lax.optimization_barrier((apply_op(start_all), precond))
    got, pre_all = lax.optimization_barrier((exchange(parts), with_edges(pre_late, 0)))
    h_raw = settle(got)
    mv, mh = pre * vec, pre * h_raw
    gram = jnp.stack(
        [
            dots(vec, vec),
            dots(vec, h_raw),
            dots(vec, mv),
            dots(vec, mh),
            dots(h_raw, mh),
            dots(mv, mv),
            dots(mv, mh),
            dots(mh, mh),
        ]
    )
    h_all = with_edges(gather(h_raw), 1)
    total = sum_all(gram)
    scale = 1.0 / jnp.sqrt(total[0] + 1e-06)
    vv, vh, vmv, vmh, hmh, mvmv, mvmh, mhmh = total * scale**2
    correlation = vmh - vh * vmv
    square = (
        mhmh
        - 2.0 * vh * mvmh
        + vh**2 * mvmv
        - 2.0 * correlation * (vmh - vh * vmv)
        + correlation**2 * vv
    )
    dir_norm = jnp.sqrt(jnp.maximum(square, 0.0) + 1e-06)
    coupling = (hmh - vh * vmh - correlation * vh) / dir_norm
    rayleigh = vh

    def direct(v, h, m):
        raw = m * (h - expand(rayleigh) * v) - expand(correlation) * v
        return raw * expand(scale / dir_norm)

    dir_all = direct(start_all.astype(F32), h_all.astype(F32), pre_all[None])
    direction = direct(vec, h_raw, pre)
    vec = vec * expand(scale)
    h_vec = h_raw * expand(scale)
    dir_bf = dir_all.astype(BF)
    got = exchange(apply_op(dir_bf))
    m_start = (pre_all[None] * start_all.astype(F32)).astype(BF)
    m_dir = (pre_all[None] * dir_bf.astype(F32)).astype(BF)
    known = [x[:, :blocks] for x in (m_start, m_dir, dir_bf, start_all)]
    h_m_start, dots_start = apply_op(m_start, known)
    h_m_dir, dots_dir = apply_op(m_dir, known)
    got, h_m_start, h_m_dir, dots_start, dots_dir = lax.optimization_barrier(
        (got, h_m_start, h_m_dir, dots_start, dots_dir)
    )
    h_dir = settle(got)

    basis = [vec, direction, h_vec, h_dir]
    weighted = [pre * x for x in basis]
    pairs = [(i, j) for i in range(4) for j in range(i, 4)]
    plain = [(0, 0), (0, 1), (1, 1), (0, 2), (0, 3), (1, 2), (1, 3)]
    gram = jnp.stack(
        [dots(basis[i], basis[j]) for i, j in plain]
        + [dots(basis[i], weighted[j]) for i, j in pairs]
        + [dots(weighted[i], weighted[j]) for i, j in pairs]
    )
    hd_all = with_edges(gather(h_dir), 1)
    m_hd = (pre_all[None] * hd_all.astype(F32)).astype(BF)
    dots_hd = apply_op(m_hd, [m_hd[:, :blocks]] + known, [h_m_start, h_m_dir], keep=False)

    def lanes(x):
        return jnp.sum(x, axis=(2, 3)) * factor

    kernel_dots = lanes(jnp.concatenate([dots_hd, dots_start, dots_dir]))
    total = sum_all(jnp.concatenate([gram, kernel_dots]))
    far = total[gram.shape[0] :]
    one = {p: total[i] for i, p in enumerate(plain)}
    first = {p: total[len(plain) + i] for i, p in enumerate(pairs)}
    second = {p: total[len(plain) + len(pairs) + i] for i, p in enumerate(pairs)}

    def form(table, left, right):
        result = 0.0
        for i, x in left:
            for j, y in right:
                result = result + x * y * table[(min(i, j), max(i, j))]
        return result

    curvature = one[(1, 3)]
    energy = 0.5 * (rayleigh + curvature) - jnp.sqrt(
        (0.5 * (rayleigh - curvature)) ** 2 + coupling**2
    )
    weight = energy - rayleigh
    size = jnp.sqrt(coupling**2 + weight**2)
    keep, mix = coupling / size, weight / size
    v_of, h_of = [(0, keep), (1, mix)], [(2, keep), (3, mix)]
    old_rayleigh, old_correlation, old_norm = rayleigh, correlation, dir_norm
    rayleigh = form(one, v_of, h_of)
    resid_of = h_of + [(i, -rayleigh * x) for i, x in v_of]
    correlation = form(first, v_of, resid_of)
    square = (
        form(second, resid_of, resid_of)
        - 2.0 * correlation * form(first, v_of, resid_of)
        + correlation**2 * form(one, v_of, v_of)
    )
    dir_norm = jnp.sqrt(jnp.maximum(square, 0.0) + 1e-06)
    coupling = (form(first, resid_of, h_of) - correlation * rayleigh) / dir_norm

    mult = [
        mix,
        scale * keep * (old_rayleigh - rayleigh),
        -rayleigh * mix,
        keep * old_norm - correlation * mix,
        scale * keep * (old_correlation - correlation),
    ]
    on_hd = far[:5]
    on_start = [far[5]] + [far[7 + i] for i in range(4)]
    on_dir = [far[6]] + [far[11 + i] for i in range(4)]
    on_d = [first[3, 3], first[0, 3] / scale, first[1, 3], one[1, 3], one[0, 3] / scale]
    on_v = [
        first[2, 3] / scale,
        first[0, 2] / scale**2,
        first[1, 2] / scale,
        one[1, 2] / scale,
        one[0, 2] / scale**2,
    ]
    curvature = 0.0
    for j, column in enumerate([on_hd, on_start, on_dir, on_d, on_v]):
        for i in range(5):
            curvature = curvature + mult[i] * mult[j] * column[i]
    curvature = curvature / dir_norm**2

    def advance(v, d, h, hd, m):
        new_v = expand(keep) * v + expand(mix) * d
        new_h = expand(keep) * h + expand(mix) * hd
        raw = m * (new_h - expand(rayleigh) * new_v) - expand(correlation) * new_v
        return new_v, raw / expand(dir_norm)

    vec, direction = advance(vec, direction, h_vec, h_dir, pre)
    energy = 0.5 * (rayleigh + curvature) - jnp.sqrt(
        (0.5 * (rayleigh - curvature)) ** 2 + coupling**2
    )
    weight = energy - rayleigh
    size = jnp.sqrt(coupling**2 + weight**2)
    final = (expand(coupling) * vec + expand(weight) * direction) / expand(size)
    return (final, energy)


def solution(mesh):
    return jax.shard_map(
        shards,
        mesh=mesh,
        in_specs=(
            P(None, "sec", None, None),
            P("term", "sec", None, None),
            P("term", "sec", None, None),
            P("term"),
            P("sec", None, None),
            P("sec"),
        ),
        out_specs=(P(None, "sec", "term", None), P()),
        check_vma=False,
    )
```

```python
import functools

import jax
import jax.numpy as jnp
from jax import lax
from jax.experimental import pallas as pl
from jax.experimental.pallas import tpu as pltpu
from jax.sharding import PartitionSpec as P

BF = jnp.bfloat16
F32 = jnp.float32
PAIRS = [(i, j) for i in range(4) for j in range(i, 4)]
PLAIN = [(0, 0), (0, 1), (1, 1), (0, 2), (0, 3), (1, 2), (1, 3)]
EXTRA = 16


def fold(product):
    rows, cols = product.shape
    tile = jnp.sum(product.reshape(rows // 8, 8, cols), axis=0)
    return sum(tile[:, i : i + 128] for i in range(0, cols, 128))


def apply_kernel(count, slot_ref, x_ref, right_ref, left_ref, *refs):
    field_refs, paired_refs, rest = refs[: count[0]], refs[count[0] : sum(count)], refs[sum(count) :]
    out_ref, z_ref = rest[0], rest[-1]
    vecs, _, states, _ = x_ref.shape
    terms, blocks = left_ref.shape[:2]
    for k in range(terms):
        for b in range(blocks):
            slot = slot_ref[k, b]
            x = x_ref[:, slot].reshape(vecs * states, states)
            z = lax.dot_general(
                x, right_ref[k, slot], (((1,), (1,)), ((), ())), preferred_element_type=F32
            ).astype(BF)
            for u in range(vecs):
                z_ref[b, pl.ds(k * states, states), pl.ds(u * states, states)] = z[
                    u * states : (u + 1) * states
                ]
    if sum(count):
        dot_ref = rest[-2]
        dot_ref[...] = jnp.zeros_like(dot_ref)
    for b in range(blocks):
        wide = jnp.concatenate([left_ref[k, b] for k in range(terms)], axis=1)
        acc = jnp.dot(wide, z_ref[b], preferred_element_type=F32)
        for u in range(vecs):
            part = acc[:, u * states : (u + 1) * states]
            if not sum(count):
                groups, share = out_ref.shape[0], out_ref.shape[3]
                out_ref[:, u, b] = part.reshape(groups, share, states).astype(out_ref.dtype)
            elif len(rest) == 3:
                out_ref[u, b] = part.astype(out_ref.dtype)
            products = [part * f[u, b].astype(F32) for f in field_refs]
            products += [x_ref[u, b].astype(F32) * f[u, b].astype(F32) for f in paired_refs]
            for i, product in enumerate(products):
                dot_ref[i, u] = dot_ref[i, u] + fold(product)


def settle_kernel(factor, got_ref, mask_ref, *refs):
    h_ref, body_ref = refs[-2:]
    groups, vecs, blocks, share, states = got_ref.shape
    row = jnp.zeros((1, 128), F32)
    lane = lax.broadcasted_iota(jnp.int32, (1, 128), 1)
    for u in range(vecs):
        tiles = [jnp.zeros((8, 128), F32) for _ in range(8)]
        for b in range(blocks):
            h = got_ref[0, u, b].astype(F32)
            for t in range(1, groups):
                h = h + got_ref[t, u, b].astype(F32)
            h = h * mask_ref[b]
            h_ref[u, b] = h
            small = h.astype(BF)
            for t in range(groups):
                body_ref[t, pl.ds((u * blocks + b) * share, share), :] = small
            if len(refs) == 4:
                v, m = refs[0][u, b].astype(F32), refs[1][b]
                mv, mh = m * v, m * h
                products = [v * v, v * h, v * mv, v * mh, h * mh, mv * mv, mv * mh, mh * mh]
                tiles = [x + fold(y) for x, y in zip(tiles, products)]
        if len(refs) == 4:
            for i, tile in enumerate(tiles):
                row = row + jnp.where(lane == i * vecs + u, jnp.sum(tile) * factor, 0.0)
    if len(refs) == 4:
        high = row.astype(BF).astype(F32)
        middle = (row - high).astype(BF).astype(F32)
        low = row - high - middle
        index = lax.broadcasted_iota(jnp.int32, (EXTRA, 128), 0)
        tile = jnp.where(index == 0, high, jnp.where(index == 1, middle, jnp.where(index == 2, low, 0.0)))
        tile = tile.astype(BF)
        for t in range(groups):
            body_ref[t, pl.ds(vecs * blocks * share, EXTRA), pl.ds(0, 128)] = tile
            body_ref[t, pl.ds(vecs * blocks * share, EXTRA), pl.ds(128, states - 128)] = jnp.zeros(
                (EXTRA, states - 128), BF
            )


def block_of(got_ref, u, b, blocks, share):
    groups, _, states = got_ref.shape
    start = (u * blocks + b) * share
    if not isinstance(start, int):
        start = pl.multiple_of(start, share)
    return got_ref[:, pl.ds(start, share), :].reshape(groups * share, states)


def unpack_kernel(core_ref, got_ref, inner_ref, outer_ref, *row_refs):
    groups = got_ref.shape[0]
    vecs, states, _ = inner_ref.shape
    share = states // groups
    core = core_ref[0]
    for u in range(vecs):
        inner_ref[u] = block_of(got_ref, u, 1 - core, 2, share)
        outer_ref[u] = block_of(got_ref, u, core, 2, share)
    for row_ref in row_refs:
        tile = jnp.zeros((EXTRA, 128), F32)
        for t in range(groups):
            tile = tile + got_ref[t, pl.ds(vecs * states * 2 // groups, EXTRA), pl.ds(0, 128)].astype(F32)
        row_ref[...] = jnp.broadcast_to(jnp.sum(tile, axis=0, keepdims=True)[None], row_ref.shape)


def slot_blocks(own_ref, core_ref, chip_ref, u, share):
    own = [block_of(own_ref, u, b, 2, share) for b in range(2)]
    return own + [core_ref[u], chip_ref[u]]


def form_kernel(coef_ref, got_ref, core_ref, chip_ref, start_ref, pre_ref, pre_core, pre_chip, dir_ref, mdir_ref):
    vecs, slots, states, _ = dir_ref.shape
    share = states // got_ref.shape[0]
    for u in range(vecs):
        hs = slot_blocks(got_ref, core_ref, chip_ref, u, share)
        for i in range(slots):
            m = (pre_ref[0], pre_ref[1], pre_core[0], pre_chip[0])[i]
            v = start_ref[u, i].astype(F32)
            raw = m * (hs[i].astype(F32) - coef_ref[0, u] * v) - coef_ref[1, u] * v
            small = (raw * coef_ref[2, u]).astype(BF)
            dir_ref[u, i] = small
            mdir_ref[u, i] = (m * small.astype(F32)).astype(BF)


def lift_kernel(got_ref, core_ref, chip_ref, pre_ref, pre_core, pre_chip, out_ref):
    vecs, slots, states, _ = out_ref.shape
    share = states // got_ref.shape[0]
    for u in range(vecs):
        hs = slot_blocks(got_ref, core_ref, chip_ref, u, share)
        for i in range(slots):
            m = (pre_ref[0], pre_ref[1], pre_core[0], pre_chip[0])[i]
            out_ref[u, i] = (m * hs[i].astype(F32)).astype(BF)


def lift_start_kernel(start_ref, pre_ref, pre_core, pre_chip, out_ref):
    vecs, slots = out_ref.shape[:2]
    for u in range(vecs):
        for i in range(slots):
            m = (pre_ref[0], pre_ref[1], pre_core[0], pre_chip[0])[i]
            out_ref[u, i] = (m * start_ref[u, i].astype(F32)).astype(BF)


def gram_kernel(coef_ref, start_ref, h_ref, hd_ref, pre_ref, dot_ref, dir_ref):
    vecs, blocks = h_ref.shape[:2]
    for u in range(vecs):
        for b in range(blocks):
            m = pre_ref[b]
            v, h = start_ref[u, b].astype(F32), h_ref[u, b]
            d = (m * (h - coef_ref[0, u] * v) - coef_ref[1, u] * v) * coef_ref[2, u]
            dir_ref[u, b] = d
            basis = [v * coef_ref[3, u], d, h * coef_ref[3, u], hd_ref[u, b]]
            lifted = [m * x for x in basis]
            products = [basis[i] * basis[j] for i, j in PLAIN]
            products += [basis[i] * lifted[j] for i, j in PAIRS]
            products += [lifted[i] * lifted[j] for i, j in PAIRS]
            for i, product in enumerate(products):
                tile = fold(product)
                dot_ref[i, u] = tile if b == 0 else dot_ref[i, u] + tile


def call(kernel, outs, args, smem=0, scratch=(), flops=0):
    vmem = pl.BlockSpec(memory_space=pltpu.VMEM)
    specs = [pl.BlockSpec(memory_space=pltpu.SMEM)] * smem + [vmem] * (len(args) - smem)
    size = sum(x.size * x.dtype.itemsize for x in list(outs) + list(args))
    return pl.pallas_call(
        kernel,
        out_shape=[jax.ShapeDtypeStruct(x.shape, x.dtype) for x in outs],
        in_specs=specs,
        out_specs=[vmem] * len(outs),
        scratch_shapes=scratch,
        compiler_params=pltpu.CompilerParams(vmem_limit_bytes=24 << 20),
        cost_estimate=pl.CostEstimate(flops=flops, bytes_accessed=size, transcendentals=0),
    )(*args)


def shards(start_vectors, left_env, right_env, term_shift, precond, block_dims):
    vecs, blocks, states, _ = start_vectors.shape
    groups = lax.axis_size("term")
    sec = lax.axis_size("sec")
    share = states // groups
    core = lax.axis_index("sec") % 2
    core_id = core.reshape(1).astype(jnp.int32)
    term = lax.axis_index("term")
    factor = 1.0 / (blocks * sec * states * states)
    position = jnp.arange(states, dtype=jnp.int32)
    live_rows = position[None, :, None] < block_dims[:, None, None]
    live_cols = position[None, None, :] < block_dims[:, None, None]
    mask = live_rows & live_cols
    shape = jax.ShapeDtypeStruct

    core_pairs = [(i, i ^ 1) for i in range(sec)]
    chip_pairs = [(i, i + 1) for i in range(1, sec - 1, 2)]
    chip_pairs = chip_pairs + [(j, i) for i, j in chip_pairs]

    def swap(inner, outer):
        return lax.ppermute(inner, "sec", core_pairs), lax.ppermute(outer, "sec", chip_pairs)

    def edges(x, axis):
        inner = lax.dynamic_index_in_dim(x, 1 - core, axis, keepdims=True)
        outer = lax.dynamic_index_in_dim(x, core, axis, keepdims=True)
        return swap(inner, outer)

    def with_edges(x, axis):
        return jnp.concatenate([x, *edges(x, axis)], axis=axis)

    def rows(x, axis):
        return lax.dynamic_slice_in_dim(x, term * share, share, axis)

    at = jnp.arange(blocks, dtype=jnp.int32)[None, :] + term_shift[:, None]
    slot = jnp.where(at < 0, 3 - core, jnp.where(at > 1, 2 + core, at)).astype(jnp.int32)

    def apply_op(x, fields=(), paired=(), keep=True):
        outs = []
        if not fields:
            outs = [shape((groups, vecs, blocks, share, states), BF)]
        elif keep:
            outs = [shape((vecs, blocks, states, states), BF)]
        count = (len(fields), len(paired))
        if sum(count):
            outs.append(shape((sum(count), vecs, 8, 128), F32))
        result = call(
            functools.partial(apply_kernel, count),
            outs,
            [slot, x, right_all, left_env, *fields, *paired],
            smem=1,
            scratch=[pltpu.VMEM((blocks, left_env.shape[0] * states, vecs * states), BF)],
            flops=16 * vecs * blocks * states**3,
        )
        return result[0] if len(outs) == 1 else result

    def exchange(parts, axis="term"):
        return lax.all_to_all(parts, axis, 0, 0)

    start = jnp.where(mask[None], start_vectors, jnp.zeros((), BF))
    right_all = with_edges(right_env, 1)
    start_all = with_edges(start, 1)
    mask_rows = rows(mask.astype(F32), 1)
    pre = rows(precond, 1)
    vec = rows(start, 2)
    slice_shape = shape((vecs, blocks, share, states), F32)
    edge_shape = shape((vecs, states, states), BF)
    four_shape = shape((vecs, 4, states, states), BF)
    lines = vecs * blocks * share

    parts, pre_late = lax.optimization_barrier((apply_op(start_all), precond))
    got = exchange(parts)
    pre_core, pre_chip = edges(pre_late, 0)
    (m_start,) = call(lift_start_kernel, [four_shape], [start_all, precond, pre_core, pre_chip])
    got, m_start, pre_core, pre_chip = lax.optimization_barrier((got, m_start, pre_core, pre_chip))

    h_raw, body = call(
        functools.partial(settle_kernel, factor),
        [slice_shape, shape((groups, lines + EXTRA, states), BF)],
        [got, mask_rows, vec, pre],
    )
    got = exchange(body)
    inner, outer, row = call(
        unpack_kernel, [edge_shape, edge_shape, shape((sec, 8, 128), F32)], [core_id, got], smem=1
    )
    h_core, h_chip = swap(inner, outer)
    row = jnp.sum(exchange(row, "sec"), axis=0)[0, : 8 * vecs]
    total = row.reshape(8, vecs)
    scale = 1.0 / jnp.sqrt(total[0] + 1e-06)
    vv, vh, vmv, vmh, hmh, mvmv, mvmh, mhmh = total * scale**2
    correlation = vmh - vh * vmv
    square = (
        mhmh
        - 2.0 * vh * mvmh
        + vh**2 * mvmv
        - 2.0 * correlation * (vmh - vh * vmv)
        + correlation**2 * vv
    )
    dir_norm = jnp.sqrt(jnp.maximum(square, 0.0) + 1e-06)
    coupling = (hmh - vh * vmh - correlation * vh) / dir_norm
    rayleigh = vh
    coef = jnp.stack([rayleigh, correlation, scale / dir_norm, scale])

    dir_all, m_dir = call(
        form_kernel,
        [four_shape, four_shape],
        [coef, got, h_core, h_chip, start_all, precond, pre_core, pre_chip],
        smem=1,
    )
    got = exchange(apply_op(dir_all))
    known = [m_start, m_dir, dir_all, start_all]
    h_m_start, dots_start = apply_op(m_start, known)
    h_m_dir, dots_dir = apply_op(m_dir, known)
    got, h_m_start, h_m_dir, dots_start, dots_dir = lax.optimization_barrier(
        (got, h_m_start, h_m_dir, dots_start, dots_dir)
    )
    h_dir, body = call(
        functools.partial(settle_kernel, factor),
        [slice_shape, shape((groups, lines, states), BF)],
        [got, mask_rows],
    )
    got = exchange(body)
    gram, direction = call(
        gram_kernel,
        [shape((len(PLAIN) + 2 * len(PAIRS), vecs, 8, 128), F32), slice_shape],
        [coef, vec, h_raw, h_dir, pre],
        smem=1,
    )
    got, gram, direction = lax.optimization_barrier((got, gram, direction))
    inner, outer = call(unpack_kernel, [edge_shape, edge_shape], [core_id, got], smem=1)
    hd_core, hd_chip = swap(inner, outer)
    (m_hd,) = call(lift_kernel, [four_shape], [got, hd_core, hd_chip, precond, pre_core, pre_chip])
    dots_hd = apply_op(m_hd, [m_hd] + known, [h_m_start, h_m_dir], keep=False)

    tiles = jnp.concatenate([gram, dots_hd, dots_start, dots_dir])
    total = jnp.sum(tiles, axis=(2, 3)) * factor
    count = total.size
    everyone = groups * sec
    row = jnp.pad(total.reshape(-1), (0, 128 - count))[None]
    row = exchange(jnp.broadcast_to(row[None], (everyone,) + row.shape), ("term", "sec"))
    total = jnp.sum(row, axis=0)[0, :count].reshape(total.shape)
    one = {p: total[i] for i, p in enumerate(PLAIN)}
    first = {p: total[len(PLAIN) + i] for i, p in enumerate(PAIRS)}
    second = {p: total[len(PLAIN) + len(PAIRS) + i] for i, p in enumerate(PAIRS)}
    far = total[gram.shape[0] :]

    def form(table, left, right):
        result = 0.0
        for i, x in left:
            for j, y in right:
                result = result + x * y * table[(min(i, j), max(i, j))]
        return result

    curvature = one[(1, 3)]
    energy = 0.5 * (rayleigh + curvature) - jnp.sqrt(
        (0.5 * (rayleigh - curvature)) ** 2 + coupling**2
    )
    weight = energy - rayleigh
    size = jnp.sqrt(coupling**2 + weight**2)
    keep, mix = coupling / size, weight / size
    v_of, h_of = [(0, keep), (1, mix)], [(2, keep), (3, mix)]
    old_rayleigh, old_correlation, old_norm = rayleigh, correlation, dir_norm
    rayleigh = form(one, v_of, h_of)
    resid_of = h_of + [(i, -rayleigh * x) for i, x in v_of]
    correlation = form(first, v_of, resid_of)
    square = (
        form(second, resid_of, resid_of)
        - 2.0 * correlation * form(first, v_of, resid_of)
        + correlation**2 * form(one, v_of, v_of)
    )
    dir_norm = jnp.sqrt(jnp.maximum(square, 0.0) + 1e-06)
    coupling = (form(first, resid_of, h_of) - correlation * rayleigh) / dir_norm

    mult = [
        mix,
        scale * keep * (old_rayleigh - rayleigh),
        -rayleigh * mix,
        keep * old_norm - correlation * mix,
        scale * keep * (old_correlation - correlation),
    ]
    on_hd = far[:5]
    on_start = [far[5]] + [far[7 + i] for i in range(4)]
    on_dir = [far[6]] + [far[11 + i] for i in range(4)]
    on_d = [first[3, 3], first[0, 3] / scale, first[1, 3], one[1, 3], one[0, 3] / scale]
    on_v = [
        first[2, 3] / scale,
        first[0, 2] / scale**2,
        first[1, 2] / scale,
        one[1, 2] / scale,
        one[0, 2] / scale**2,
    ]
    curvature = 0.0
    for j, column in enumerate([on_hd, on_start, on_dir, on_d, on_v]):
        for i in range(5):
            curvature = curvature + mult[i] * mult[j] * column[i]
    curvature = curvature / dir_norm**2
    energy = 0.5 * (rayleigh + curvature) - jnp.sqrt(
        (0.5 * (rayleigh - curvature)) ** 2 + coupling**2
    )
    weight = energy - rayleigh
    size = jnp.sqrt(coupling**2 + weight**2)

    def expand(value):
        return value[:, None, None, None]

    new_v = expand(keep * scale) * vec.astype(F32) + expand(mix) * direction
    new_h = expand(keep * scale) * h_raw + expand(mix) * h_dir
    raw = pre[None] * (new_h - expand(rayleigh) * new_v) - expand(correlation) * new_v
    final = expand(coupling / size) * new_v + expand(weight / (dir_norm * size)) * raw
    return (final, energy)


def solution(mesh):
    return jax.shard_map(
        shards,
        mesh=mesh,
        in_specs=(
            P(None, "sec", None, None),
            P("term", "sec", None, None),
            P("term", "sec", None, None),
            P("term"),
            P("sec", None, None),
            P("sec"),
        ),
        out_specs=(P(None, "sec", "term", None), P()),
        check_vma=False,
    )
```

```python
import functools

import jax
import jax.numpy as jnp
from jax import lax
from jax.experimental import pallas as pl
from jax.experimental.pallas import tpu as pltpu
from jax.sharding import PartitionSpec as P


BF = jnp.bfloat16
F32 = jnp.float32
PAIRS = [(i, j) for i in range(4) for j in range(i, 4)]
PLAIN = [(0, 0), (0, 1), (1, 1), (0, 2), (0, 3), (1, 2), (1, 3)]
EXTRA = 16


def fold(product):
    rows, cols = product.shape
    tile = jnp.sum(product.reshape(rows // 8, 8, cols), axis=0)
    return sum(tile[:, i : i + 128] for i in range(0, cols, 128))


def apply_kernel(count, slot_ref, x_ref, right_ref, left_ref, *refs):
    field_refs, paired_refs, rest = refs[: count[0]], refs[count[0] : sum(count)], refs[sum(count) :]
    out_ref, z_ref = rest[0], rest[-1]
    vecs, _, states, _ = x_ref.shape
    terms, blocks = left_ref.shape[:2]
    for k in range(terms):
        for b in range(blocks):
            slot = slot_ref[k, b]
            x = x_ref[:, slot].reshape(vecs * states, states)
            z = lax.dot_general(
                x, right_ref[k, slot], (((1,), (1,)), ((), ())), preferred_element_type=F32
            ).astype(BF)
            for u in range(vecs):
                z_ref[b, pl.ds(k * states, states), pl.ds(u * states, states)] = z[
                    u * states : (u + 1) * states
                ]
    if sum(count):
        dot_ref = rest[-2]
        dot_ref[...] = jnp.zeros_like(dot_ref)
    for b in range(blocks):
        wide = jnp.concatenate([left_ref[k, b] for k in range(terms)], axis=1)
        acc = jnp.dot(wide, z_ref[b], preferred_element_type=F32)
        for u in range(vecs):
            part = acc[:, u * states : (u + 1) * states]
            if not sum(count):
                groups, share = out_ref.shape[0], out_ref.shape[3]
                out_ref[:, u, b] = part.reshape(groups, share, states).astype(out_ref.dtype)
            elif len(rest) == 3:
                out_ref[u, b] = part.astype(out_ref.dtype)
            products = [part * f[u, b].astype(F32) for f in field_refs]
            products += [x_ref[u, b].astype(F32) * f[u, b].astype(F32) for f in paired_refs]
            for i, product in enumerate(products):
                dot_ref[i, u] = dot_ref[i, u] + fold(product)


def settle_kernel(factor, got_ref, mask_ref, *refs):
    h_ref, body_ref = refs[-2:]
    groups, vecs, blocks, share, states = got_ref.shape
    row = jnp.zeros((1, 128), F32)
    lane = lax.broadcasted_iota(jnp.int32, (1, 128), 1)
    for u in range(vecs):
        tiles = [jnp.zeros((8, 128), F32) for _ in range(8)]
        for b in range(blocks):
            h = got_ref[0, u, b].astype(F32)
            for t in range(1, groups):
                h = h + got_ref[t, u, b].astype(F32)
            h = h * mask_ref[b]
            h_ref[u, b] = h
            small = h.astype(BF)
            for t in range(groups):
                body_ref[t, pl.ds((u * blocks + b) * share, share), :] = small
            if len(refs) == 4:
                v, m = refs[0][u, b].astype(F32), refs[1][b]
                mv, mh = m * v, m * h
                products = [v * v, v * h, v * mv, v * mh, h * mh, mv * mv, mv * mh, mh * mh]
                tiles = [x + fold(y) for x, y in zip(tiles, products)]
        if len(refs) == 4:
            for i, tile in enumerate(tiles):
                row = row + jnp.where(lane == i * vecs + u, jnp.sum(tile) * factor, 0.0)
    if len(refs) == 4:
        high = row.astype(BF).astype(F32)
        middle = (row - high).astype(BF).astype(F32)
        low = row - high - middle
        index = lax.broadcasted_iota(jnp.int32, (EXTRA, 128), 0)
        tile = jnp.where(index == 0, high, jnp.where(index == 1, middle, jnp.where(index == 2, low, 0.0)))
        tile = tile.astype(BF)
        for t in range(groups):
            body_ref[t, pl.ds(vecs * blocks * share, EXTRA), pl.ds(0, 128)] = tile
            body_ref[t, pl.ds(vecs * blocks * share, EXTRA), pl.ds(128, states - 128)] = jnp.zeros(
                (EXTRA, states - 128), BF
            )


def block_of(got_ref, u, b, blocks, share):
    groups, _, states = got_ref.shape
    start = (u * blocks + b) * share
    if not isinstance(start, int):
        start = pl.multiple_of(start, share)
    return got_ref[:, pl.ds(start, share), :].reshape(groups * share, states)


def unpack_kernel(core_ref, got_ref, inner_ref, outer_ref, *row_refs):
    groups = got_ref.shape[0]
    vecs, states, _ = inner_ref.shape
    share = states // groups
    core = core_ref[0]
    for u in range(vecs):
        inner_ref[u] = block_of(got_ref, u, 1 - core, 2, share)
        outer_ref[u] = block_of(got_ref, u, core, 2, share)
    for row_ref in row_refs:
        tile = jnp.zeros((EXTRA, 128), F32)
        for t in range(groups):
            tile = tile + got_ref[t, pl.ds(vecs * states * 2 // groups, EXTRA), pl.ds(0, 128)].astype(F32)
        row_ref[...] = jnp.broadcast_to(jnp.sum(tile, axis=0, keepdims=True)[None], row_ref.shape)


def slot_blocks(own_ref, core_ref, chip_ref, u, share):
    own = [block_of(own_ref, u, b, 2, share) for b in range(2)]
    return own + [core_ref[u], chip_ref[u]]


def form_kernel(row_ref, got_ref, core_ref, chip_ref, start_ref, pre_ref, pre_core, pre_chip, dir_ref, mdir_ref, coef_ref):
    vecs, slots, states, _ = dir_ref.shape
    share = states // got_ref.shape[0]
    row = row_ref[0]
    for i in range(1, row_ref.shape[0]):
        row = row + row_ref[i]
    row = row[0:1]
    lane = lax.broadcasted_iota(jnp.int32, row.shape, 1)
    index = lax.broadcasted_iota(jnp.int32, coef_ref.shape, 0)
    lanes = lax.broadcasted_iota(jnp.int32, coef_ref.shape, 1)
    table = jnp.zeros(coef_ref.shape, F32)
    for u in range(vecs):
        total = [
            jnp.sum(jnp.where(lane == i * vecs + u, row, 0.0), axis=1, keepdims=True)
            for i in range(8)
        ]
        scale = 1.0 / jnp.sqrt(total[0] + 1e-06)
        vv, vh, vmv, vmh, hmh, mvmv, mvmh, mhmh = [x * (scale * scale) for x in total]
        correlation = vmh - vh * vmv
        square = mhmh - 2.0 * vh * mvmh + vh * vh * mvmv
        square = square - 2.0 * correlation * (vmh - vh * vmv) + correlation * correlation * vv
        norm = jnp.sqrt(jnp.maximum(square, 0.0) + 1e-06)
        coupling = (hmh - vh * vmh - correlation * vh) / norm
        alpha = scale / norm
        for j, x in enumerate([vh, correlation, alpha, scale, coupling, norm]):
            table = table + jnp.where((index == j) & (lanes == u), x, 0.0)
        hs = slot_blocks(got_ref, core_ref, chip_ref, u, share)
        for i in range(slots):
            m = (pre_ref[0], pre_ref[1], pre_core[0], pre_chip[0])[i]
            v = start_ref[u, i].astype(F32)
            raw = m * (hs[i].astype(F32) - vh * v) - correlation * v
            small = (raw * alpha).astype(BF)
            dir_ref[u, i] = small
            mdir_ref[u, i] = (m * small.astype(F32)).astype(BF)
    coef_ref[...] = table


def lift_kernel(got_ref, core_ref, chip_ref, pre_ref, pre_core, pre_chip, out_ref):
    vecs, slots, states, _ = out_ref.shape
    share = states // got_ref.shape[0]
    for u in range(vecs):
        hs = slot_blocks(got_ref, core_ref, chip_ref, u, share)
        for i in range(slots):
            m = (pre_ref[0], pre_ref[1], pre_core[0], pre_chip[0])[i]
            out_ref[u, i] = (m * hs[i].astype(F32)).astype(BF)


def lift_start_kernel(start_ref, pre_ref, pre_core, pre_chip, out_ref):
    vecs, slots = out_ref.shape[:2]
    for u in range(vecs):
        for i in range(slots):
            m = (pre_ref[0], pre_ref[1], pre_core[0], pre_chip[0])[i]
            out_ref[u, i] = (m * start_ref[u, i].astype(F32)).astype(BF)


def gram_kernel(coef_ref, start_ref, h_ref, hd_ref, pre_ref, dot_ref, dir_ref):
    vecs, blocks = h_ref.shape[:2]
    for u in range(vecs):
        rayleigh, correlation, alpha, scale = [coef_ref[j : j + 1, u : u + 1] for j in range(4)]
        for b in range(blocks):
            m = pre_ref[b]
            v, h = start_ref[u, b].astype(F32), h_ref[u, b]
            d = (m * (h - rayleigh * v) - correlation * v) * alpha
            dir_ref[u, b] = d
            basis = [v * scale, d, h * scale, hd_ref[u, b]]
            lifted = [m * x for x in basis]
            products = [basis[i] * basis[j] for i, j in PLAIN]
            products += [basis[i] * lifted[j] for i, j in PAIRS]
            products += [lifted[i] * lifted[j] for i, j in PAIRS]
            for i, product in enumerate(products):
                tile = fold(product)
                dot_ref[i, u] = tile if b == 0 else dot_ref[i, u] + tile


def call(kernel, outs, args, smem=0, scratch=(), flops=0):
    vmem = pl.BlockSpec(memory_space=pltpu.VMEM)
    specs = [pl.BlockSpec(memory_space=pltpu.SMEM)] * smem + [vmem] * (len(args) - smem)
    size = sum(x.size * x.dtype.itemsize for x in list(outs) + list(args))
    return pl.pallas_call(
        kernel,
        out_shape=[jax.ShapeDtypeStruct(x.shape, x.dtype) for x in outs],
        in_specs=specs,
        out_specs=[vmem] * len(outs),
        scratch_shapes=scratch,
        compiler_params=pltpu.CompilerParams(vmem_limit_bytes=24 << 20),
        cost_estimate=pl.CostEstimate(flops=flops, bytes_accessed=size, transcendentals=0),
    )(*args)


def shards(start_vectors, left_env, right_env, term_shift, precond, block_dims):
    vecs, blocks, states, _ = start_vectors.shape
    groups = lax.axis_size("term")
    sec = lax.axis_size("sec")
    share = states // groups
    core = lax.axis_index("sec") % 2
    core_id = core.reshape(1).astype(jnp.int32)
    term = lax.axis_index("term")
    factor = 1.0 / (blocks * sec * states * states)
    position = jnp.arange(states, dtype=jnp.int32)
    live_rows = position[None, :, None] < block_dims[:, None, None]
    live_cols = position[None, None, :] < block_dims[:, None, None]
    mask = live_rows & live_cols
    shape = jax.ShapeDtypeStruct

    core_pairs = [(i, i ^ 1) for i in range(sec)]
    chip_pairs = [(i, i + 1) for i in range(1, sec - 1, 2)]
    chip_pairs = chip_pairs + [(j, i) for i, j in chip_pairs]

    def swap(inner, outer):
        outer = lax.ppermute(outer, "sec", chip_pairs)
        inner = lax.ppermute(inner, "sec", core_pairs)
        return inner, outer

    def edges(x, axis):
        inner = lax.dynamic_index_in_dim(x, 1 - core, axis, keepdims=True)
        outer = lax.dynamic_index_in_dim(x, core, axis, keepdims=True)
        return inner, outer

    def rows(x, axis):
        return lax.dynamic_slice_in_dim(x, term * share, share, axis)

    at = jnp.arange(blocks, dtype=jnp.int32)[None, :] + term_shift[:, None]
    slot = jnp.where(at < 0, 3 - core, jnp.where(at > 1, 2 + core, at)).astype(jnp.int32)

    def apply_op(x, fields=(), paired=(), keep=True):
        outs = []
        if not fields:
            outs = [shape((groups, vecs, blocks, share, states), BF)]
        elif keep:
            outs = [shape((vecs, blocks, states, states), BF)]
        count = (len(fields), len(paired))
        if sum(count):
            outs.append(shape((sum(count), vecs, 8, 128), F32))
        result = call(
            functools.partial(apply_kernel, count),
            outs,
            [slot, x, right_all, left_env, *fields, *paired],
            smem=1,
            scratch=[pltpu.VMEM((blocks, left_env.shape[0] * states, vecs * states), BF)],
            flops=16 * vecs * blocks * states**3,
        )
        return result[0] if len(outs) == 1 else result

    def exchange(parts, axis="term"):
        return lax.all_to_all(parts, axis, 0, 0)

    barrier = lax.optimization_barrier

    slice_shape = shape((vecs, blocks, share, states), F32)
    edge_shape = shape((vecs, states, states), BF)
    four_shape = shape((vecs, 4, states, states), BF)
    lines = vecs * blocks * share

    right_all = jnp.concatenate([right_env, *swap(*edges(right_env, 1))], axis=1)
    start = jnp.where(mask[None], start_vectors, jnp.zeros((), BF))
    start_all = jnp.concatenate([start, *swap(*edges(start, 1))], axis=1)
    early = (rows(mask.astype(F32), 1), rows(precond, 1), rows(start, 2), *edges(precond, 0))
    start_all, right_all, early = barrier((start_all, right_all, early))
    mask_rows, pre, vec, pre_inner, pre_outer = early

    parts, pre_inner, pre_outer = barrier((apply_op(start_all), pre_inner, pre_outer))
    pre_core, pre_chip = swap(pre_inner, pre_outer)
    got = exchange(parts)
    h_raw, body = call(
        functools.partial(settle_kernel, factor),
        [slice_shape, shape((groups, lines + EXTRA, states), BF)],
        [got, mask_rows, vec, pre],
    )
    got = exchange(body)
    inner, outer, row = call(
        unpack_kernel, [edge_shape, edge_shape, shape((sec, 8, 128), F32)], [core_id, got], smem=1
    )
    h_core, h_chip = swap(inner, outer)
    row = exchange(row, "sec")
    row, pre_core, pre_chip = barrier((row, pre_core, pre_chip))
    dir_all, m_dir, coef = call(
        form_kernel,
        [four_shape, four_shape, shape((16, 128), F32)],
        [row, got, h_core, h_chip, start_all, precond, pre_core, pre_chip],
    )
    parts, dir_all, m_dir = barrier((apply_op(dir_all), dir_all, m_dir))
    got = exchange(parts)
    h_dir, body = call(
        functools.partial(settle_kernel, factor),
        [slice_shape, shape((groups, lines, states), BF)],
        [got, mask_rows],
    )
    got = exchange(body)
    got, h_dir, m_dir, start_all = barrier((got, h_dir, m_dir, start_all))
    inner, outer = call(unpack_kernel, [edge_shape, edge_shape], [core_id, got], smem=1)
    hd_core, hd_chip = swap(inner, outer)
    (m_start,) = call(lift_start_kernel, [four_shape], [start_all, precond, pre_core, pre_chip])
    known = [m_start, m_dir, dir_all, start_all]
    h_m_start, dots_start = apply_op(m_start, known)
    h_m_dir, dots_dir = apply_op(m_dir, known)
    gram, direction = call(
        gram_kernel,
        [shape((len(PLAIN) + 2 * len(PAIRS), vecs, 8, 128), F32), slice_shape],
        [coef, vec, h_raw, h_dir, pre],
    )
    (m_hd,) = call(lift_kernel, [four_shape], [got, hd_core, hd_chip, precond, pre_core, pre_chip])
    dots_hd = apply_op(m_hd, [m_hd] + known, [h_m_start, h_m_dir], keep=False)
    rayleigh, correlation, _, scale, coupling, dir_norm = [coef[j, :vecs] for j in range(6)]

    tiles = jnp.concatenate([gram, dots_hd, dots_start, dots_dir])
    total = jnp.sum(tiles, axis=(2, 3)) * factor
    count = total.size
    everyone = groups * sec
    row = jnp.pad(total.reshape(-1), (0, 128 - count))[None]
    row = jnp.broadcast_to(row[None], (everyone,) + row.shape)
    row = exchange(row, ("term", "sec"))
    total = jnp.sum(row, axis=0)[0, :count].reshape(total.shape)
    one = {p: total[i] for i, p in enumerate(PLAIN)}
    first = {p: total[len(PLAIN) + i] for i, p in enumerate(PAIRS)}
    second = {p: total[len(PLAIN) + len(PAIRS) + i] for i, p in enumerate(PAIRS)}
    far = total[gram.shape[0] :]

    def form(table, left, right):
        result = 0.0
        for i, x in left:
            for j, y in right:
                result = result + x * y * table[(min(i, j), max(i, j))]
        return result

    curvature = one[(1, 3)]
    energy = 0.5 * (rayleigh + curvature) - jnp.sqrt(
        (0.5 * (rayleigh - curvature)) ** 2 + coupling**2
    )
    weight = energy - rayleigh
    size = jnp.sqrt(coupling**2 + weight**2)
    keep, mix = coupling / size, weight / size
    v_of, h_of = [(0, keep), (1, mix)], [(2, keep), (3, mix)]
    old_rayleigh, old_correlation, old_norm = rayleigh, correlation, dir_norm
    rayleigh = form(one, v_of, h_of)
    resid_of = h_of + [(i, -rayleigh * x) for i, x in v_of]
    correlation = form(first, v_of, resid_of)
    square = (
        form(second, resid_of, resid_of)
        - 2.0 * correlation * form(first, v_of, resid_of)
        + correlation**2 * form(one, v_of, v_of)
    )
    dir_norm = jnp.sqrt(jnp.maximum(square, 0.0) + 1e-06)
    coupling = (form(first, resid_of, h_of) - correlation * rayleigh) / dir_norm

    mult = [
        mix,
        scale * keep * (old_rayleigh - rayleigh),
        -rayleigh * mix,
        keep * old_norm - correlation * mix,
        scale * keep * (old_correlation - correlation),
    ]
    on_hd = far[:5]
    on_start = [far[5]] + [far[7 + i] for i in range(4)]
    on_dir = [far[6]] + [far[11 + i] for i in range(4)]
    on_d = [first[3, 3], first[0, 3] / scale, first[1, 3], one[1, 3], one[0, 3] / scale]
    on_v = [
        first[2, 3] / scale,
        first[0, 2] / scale**2,
        first[1, 2] / scale,
        one[1, 2] / scale,
        one[0, 2] / scale**2,
    ]
    curvature = 0.0
    for j, column in enumerate([on_hd, on_start, on_dir, on_d, on_v]):
        for i in range(5):
            curvature = curvature + mult[i] * mult[j] * column[i]
    curvature = curvature / dir_norm**2
    energy = 0.5 * (rayleigh + curvature) - jnp.sqrt(
        (0.5 * (rayleigh - curvature)) ** 2 + coupling**2
    )
    weight = energy - rayleigh
    size = jnp.sqrt(coupling**2 + weight**2)

    def expand(value):
        return value[:, None, None, None]

    new_v = expand(keep * scale) * vec.astype(F32) + expand(mix) * direction
    new_h = expand(keep * scale) * h_raw + expand(mix) * h_dir
    raw = pre[None] * (new_h - expand(rayleigh) * new_v) - expand(correlation) * new_v
    final = expand(coupling / size) * new_v + expand(weight / (dir_norm * size)) * raw
    return (final, energy)


def solution(mesh):
    return jax.shard_map(
        shards,
        mesh=mesh,
        in_specs=(
            P(None, "sec", None, None),
            P("term", "sec", None, None),
            P("term", "sec", None, None),
            P("term"),
            P("sec", None, None),
            P("sec"),
        ),
        out_specs=(P(None, "sec", "term", None), P()),
        check_vma=False,
    )
```

```python
import functools

import jax
import jax.numpy as jnp
from jax import lax
from jax.experimental import pallas as pl
from jax.experimental.pallas import tpu as pltpu
from jax.sharding import PartitionSpec as P


BF = jnp.bfloat16
F32 = jnp.float32
PAIRS = [(i, j) for i in range(4) for j in range(i, 4)]
PLAIN = [(0, 0), (0, 1), (1, 1), (0, 2), (0, 3), (1, 2), (1, 3)]
EXTRA = 16


def fold(product):
    rows, cols = product.shape
    tile = jnp.sum(product.reshape(rows // 8, 8, cols), axis=0)
    return sum(tile[:, i : i + 128] for i in range(0, cols, 128))


def apply_kernel(count, slot_ref, x_ref, right_ref, left_ref, *refs):
    field_refs, paired_refs, rest = refs[: count[0]], refs[count[0] : sum(count)], refs[sum(count) :]
    out_ref, z_ref = rest[0], rest[-1]
    vecs, _, states, _ = x_ref.shape
    terms, blocks = left_ref.shape[:2]
    for k in range(terms):
        for b in range(blocks):
            slot = slot_ref[k, b]
            x = x_ref[:, slot].reshape(vecs * states, states)
            z = lax.dot_general(
                x, right_ref[k, slot], (((1,), (1,)), ((), ())), preferred_element_type=F32
            ).astype(BF)
            for u in range(vecs):
                z_ref[b, pl.ds(k * states, states), pl.ds(u * states, states)] = z[
                    u * states : (u + 1) * states
                ]
    if sum(count):
        dot_ref = rest[-2]
        dot_ref[...] = jnp.zeros_like(dot_ref)
    for b in range(blocks):
        wide = jnp.concatenate([left_ref[k, b] for k in range(terms)], axis=1)
        acc = jnp.dot(wide, z_ref[b], preferred_element_type=F32)
        for u in range(vecs):
            part = acc[:, u * states : (u + 1) * states]
            if not sum(count):
                groups, share = out_ref.shape[0], out_ref.shape[3]
                out_ref[:, u, b] = part.reshape(groups, share, states).astype(out_ref.dtype)
            elif len(rest) == 3:
                out_ref[u, b] = part.astype(out_ref.dtype)
            products = [part * f[u, b].astype(F32) for f in field_refs]
            products += [x_ref[u, b].astype(F32) * f[u, b].astype(F32) for f in paired_refs]
            for i, product in enumerate(products):
                dot_ref[i, u] = dot_ref[i, u] + fold(product)


def settle_kernel(factor, got_ref, mask_ref, *refs):
    h_ref, body_ref = refs[-2:]
    groups, vecs, blocks, share, states = got_ref.shape
    row = jnp.zeros((1, 128), F32)
    lane = lax.broadcasted_iota(jnp.int32, (1, 128), 1)
    for u in range(vecs):
        tiles = [jnp.zeros((8, 128), F32) for _ in range(8)]
        for b in range(blocks):
            h = got_ref[0, u, b].astype(F32)
            for t in range(1, groups):
                h = h + got_ref[t, u, b].astype(F32)
            h = h * mask_ref[b]
            h_ref[u, b] = h
            small = h.astype(BF)
            for t in range(groups):
                body_ref[t, pl.ds((u * blocks + b) * share, share), :] = small
            if len(refs) == 4:
                v, m = refs[0][u, b].astype(F32), refs[1][b]
                mv, mh = m * v, m * h
                products = [v * v, v * h, v * mv, v * mh, h * mh, mv * mv, mv * mh, mh * mh]
                tiles = [x + fold(y) for x, y in zip(tiles, products)]
        if len(refs) == 4:
            for i, tile in enumerate(tiles):
                row = row + jnp.where(lane == i * vecs + u, jnp.sum(tile) * factor, 0.0)
    if len(refs) == 4:
        high = row.astype(BF).astype(F32)
        middle = (row - high).astype(BF).astype(F32)
        low = row - high - middle
        index = lax.broadcasted_iota(jnp.int32, (EXTRA, 128), 0)
        tile = jnp.where(index == 0, high, jnp.where(index == 1, middle, jnp.where(index == 2, low, 0.0)))
        tile = tile.astype(BF)
        for t in range(groups):
            body_ref[t, pl.ds(vecs * blocks * share, EXTRA), pl.ds(0, 128)] = tile
            body_ref[t, pl.ds(vecs * blocks * share, EXTRA), pl.ds(128, states - 128)] = jnp.zeros(
                (EXTRA, states - 128), BF
            )


def block_of(got_ref, u, b, blocks, share):
    groups, _, states = got_ref.shape
    start = (u * blocks + b) * share
    if not isinstance(start, int):
        start = pl.multiple_of(start, share)
    return got_ref[:, pl.ds(start, share), :].reshape(groups * share, states)


def unpack_kernel(core_ref, got_ref, inner_ref, outer_ref, *row_refs):
    groups = got_ref.shape[0]
    vecs, states, _ = inner_ref.shape
    share = states // groups
    core = core_ref[0]
    for u in range(vecs):
        inner_ref[u] = block_of(got_ref, u, 1 - core, 2, share)
        outer_ref[u] = block_of(got_ref, u, core, 2, share)
    for row_ref in row_refs:
        tile = jnp.zeros((EXTRA, 128), F32)
        for t in range(groups):
            tile = tile + got_ref[t, pl.ds(vecs * states * 2 // groups, EXTRA), pl.ds(0, 128)].astype(F32)
        row_ref[...] = jnp.broadcast_to(jnp.sum(tile, axis=0, keepdims=True)[None], row_ref.shape)


def slot_blocks(own_ref, core_ref, chip_ref, u, share):
    own = [block_of(own_ref, u, b, 2, share) for b in range(2)]
    return own + [core_ref[u], chip_ref[u]]


def pick(row, i, vecs):
    return row if i == 0 else pltpu.roll(row, 128 - i * vecs, 1)


def lane_of(row, u):
    lane = lax.broadcasted_iota(jnp.int32, row.shape, 1)
    return jnp.sum(jnp.where(lane == u, row, 0.0), axis=1, keepdims=True)


def form_kernel(row_ref, got_ref, core_ref, chip_ref, start_ref, pre_ref, pre_core, pre_chip, dir_ref, mdir_ref, coef_ref):
    vecs, slots, states, _ = dir_ref.shape
    share = states // got_ref.shape[0]
    row = row_ref[0]
    for i in range(1, row_ref.shape[0]):
        row = row + row_ref[i]
    total = [pick(row, i, vecs) for i in range(8)]
    scale = 1.0 / jnp.sqrt(total[0] + 1e-06)
    vv, vh, vmv, vmh, hmh, mvmv, mvmh, mhmh = [x * (scale * scale) for x in total]
    correlation = vmh - vh * vmv
    square = mhmh - 2.0 * vh * mvmh + vh * vh * mvmv
    square = square - 2.0 * correlation * (vmh - vh * vmv) + correlation * correlation * vv
    norm = jnp.sqrt(jnp.maximum(square, 0.0) + 1e-06)
    coupling = (hmh - vh * vmh - correlation * vh) / norm
    alpha = scale / norm
    for j, x in enumerate([vh, correlation, alpha, scale, coupling, norm]):
        coef_ref[j] = x
    for u in range(vecs):
        ray, corr, mult = [lane_of(x[0:1], u) for x in (vh, correlation, alpha)]
        hs = slot_blocks(got_ref, core_ref, chip_ref, u, share)
        for i in range(slots):
            m = (pre_ref[0], pre_ref[1], pre_core[0], pre_chip[0])[i]
            v = start_ref[u, i].astype(F32)
            raw = m * (hs[i].astype(F32) - ray * v) - corr * v
            small = (raw * mult).astype(BF)
            dir_ref[u, i] = small
            mdir_ref[u, i] = (m * small.astype(F32)).astype(BF)


def lift_kernel(got_ref, core_ref, chip_ref, pre_ref, pre_core, pre_chip, out_ref):
    vecs, slots, states, _ = out_ref.shape
    share = states // got_ref.shape[0]
    for u in range(vecs):
        hs = slot_blocks(got_ref, core_ref, chip_ref, u, share)
        for i in range(slots):
            m = (pre_ref[0], pre_ref[1], pre_core[0], pre_chip[0])[i]
            out_ref[u, i] = (m * hs[i].astype(F32)).astype(BF)


def lift_start_kernel(start_ref, pre_ref, pre_core, pre_chip, out_ref):
    vecs, slots = out_ref.shape[:2]
    for u in range(vecs):
        for i in range(slots):
            m = (pre_ref[0], pre_ref[1], pre_core[0], pre_chip[0])[i]
            out_ref[u, i] = (m * start_ref[u, i].astype(F32)).astype(BF)


def gram_kernel(coef_ref, start_ref, h_ref, hd_ref, pre_ref, dot_ref, dir_ref):
    vecs, blocks = h_ref.shape[:2]
    for u in range(vecs):
        rayleigh, correlation, alpha, scale = [lane_of(coef_ref[j, 0:1], u) for j in range(4)]
        for b in range(blocks):
            m = pre_ref[b]
            v, h = start_ref[u, b].astype(F32), h_ref[u, b]
            d = (m * (h - rayleigh * v) - correlation * v) * alpha
            dir_ref[u, b] = d
            basis = [v * scale, d, h * scale, hd_ref[u, b]]
            lifted = [m * x for x in basis]
            products = [basis[i] * basis[j] for i, j in PLAIN]
            products += [basis[i] * lifted[j] for i, j in PAIRS]
            products += [lifted[i] * lifted[j] for i, j in PAIRS]
            for i, product in enumerate(products):
                tile = fold(product)
                dot_ref[i, u] = tile if b == 0 else dot_ref[i, u] + tile


def tally_kernel(factor, *refs):
    out_ref = refs[-1]
    lines = []
    for ref in refs[:-1]:
        for i in range(ref.shape[0]):
            lines += [jnp.sum(ref[i, u], axis=0, keepdims=True) for u in range(ref.shape[1])]
    lines.append(jnp.zeros((128 - len(lines), 128), F32))
    table = jnp.concatenate(lines, axis=0)
    row = lax.dot_general(
        jnp.ones((8, 128), F32),
        table,
        (((1,), (1,)), ((), ())),
        precision=lax.Precision.HIGHEST,
        preferred_element_type=F32,
    )
    out_ref[...] = jnp.broadcast_to((row[0:1] * factor)[None], out_ref.shape)


def form(table, left, right):
    result = None
    for i, x in left:
        for j, y in right:
            term = x * y * table[(min(i, j), max(i, j))]
            result = term if result is None else result + term
    return result


def lowest(rayleigh, curvature, coupling):
    half = 0.5 * (rayleigh - curvature)
    energy = 0.5 * (rayleigh + curvature) - jnp.sqrt(half * half + coupling * coupling)
    weight = energy - rayleigh
    return energy, weight, jnp.sqrt(coupling * coupling + weight * weight)


def finish_kernel(row_ref, coef_ref, start_ref, dir_ref, h_ref, hd_ref, pre_ref, out_ref, energy_ref):
    vecs, blocks = out_ref.shape[:2]
    row = row_ref[0]
    for i in range(1, row_ref.shape[0]):
        row = row + row_ref[i]
    count = len(PLAIN) + 2 * len(PAIRS) + 15
    total = [pick(row, i, vecs) for i in range(count)]
    one = {p: total[i] for i, p in enumerate(PLAIN)}
    first = {p: total[len(PLAIN) + i] for i, p in enumerate(PAIRS)}
    second = {p: total[len(PLAIN) + len(PAIRS) + i] for i, p in enumerate(PAIRS)}
    far = total[len(PLAIN) + 2 * len(PAIRS) :]
    old_ray, old_corr, _, scale, coupling, old_norm = [coef_ref[j, 0:1] for j in range(6)]

    _, weight, size = lowest(old_ray, one[(1, 3)], coupling)
    keep, mix = coupling / size, weight / size
    v_of, h_of = [(0, keep), (1, mix)], [(2, keep), (3, mix)]
    rayleigh = form(one, v_of, h_of)
    resid_of = h_of + [(i, -rayleigh * x) for i, x in v_of]
    correlation = form(first, v_of, resid_of)
    square = form(second, resid_of, resid_of) - 2.0 * correlation * form(first, v_of, resid_of)
    square = square + correlation * correlation * form(one, v_of, v_of)
    norm = jnp.sqrt(jnp.maximum(square, 0.0) + 1e-06)
    coupling = (form(first, resid_of, h_of) - correlation * rayleigh) / norm

    mult = [
        mix,
        scale * keep * (old_ray - rayleigh),
        -rayleigh * mix,
        keep * old_norm - correlation * mix,
        scale * keep * (old_corr - correlation),
    ]
    back = 1.0 / scale
    on_hd = far[:5]
    on_start = [far[5]] + [far[7 + i] for i in range(4)]
    on_dir = [far[6]] + [far[11 + i] for i in range(4)]
    on_d = [first[3, 3], first[0, 3] * back, first[1, 3], one[1, 3], one[0, 3] * back]
    on_v = [first[2, 3], first[0, 2] * back, first[1, 2], one[1, 2], one[0, 2] * back]
    curvature = None
    for j, column in enumerate([on_hd, on_start, on_dir, on_d, on_v]):
        line = None
        for i in range(5):
            term = mult[i] * column[i]
            line = term if line is None else line + term
        line = line * (mult[j] * back if j == 4 else mult[j])
        curvature = line if curvature is None else curvature + line
    curvature = curvature / (norm * norm)
    energy, weight, size = lowest(rayleigh, curvature, coupling)
    of_v, of_raw = coupling / size, weight / (norm * size)
    values = (keep * scale, mix, rayleigh, correlation, of_v, of_raw)
    for u in range(vecs):
        energy_ref[u] = lane_of(energy, u)[0, 0]
        first_v, then_d, ray, corr, use_v, use_raw = [lane_of(x, u) for x in values]
        for b in range(blocks):
            new_v = first_v * start_ref[u, b].astype(F32) + then_d * dir_ref[u, b]
            new_h = first_v * h_ref[u, b] + then_d * hd_ref[u, b]
            raw = pre_ref[b] * (new_h - ray * new_v) - corr * new_v
            out_ref[u, b] = use_v * new_v + use_raw * raw


def call(kernel, outs, args, smem=0, scratch=(), flops=0, smem_outs=0):
    vmem = pl.BlockSpec(memory_space=pltpu.VMEM)
    specs = [pl.BlockSpec(memory_space=pltpu.SMEM)] * smem + [vmem] * (len(args) - smem)
    size = sum(x.size * x.dtype.itemsize for x in list(outs) + list(args))
    return pl.pallas_call(
        kernel,
        out_shape=[jax.ShapeDtypeStruct(x.shape, x.dtype) for x in outs],
        in_specs=specs,
        out_specs=[vmem] * (len(outs) - smem_outs)
        + [pl.BlockSpec(memory_space=pltpu.SMEM)] * smem_outs,
        scratch_shapes=scratch,
        compiler_params=pltpu.CompilerParams(vmem_limit_bytes=24 << 20),
        cost_estimate=pl.CostEstimate(flops=flops, bytes_accessed=size, transcendentals=0),
    )(*args)


def shards(start_vectors, left_env, right_env, term_shift, precond, block_dims):
    vecs, blocks, states, _ = start_vectors.shape
    groups = lax.axis_size("term")
    sec = lax.axis_size("sec")
    share = states // groups
    core = lax.axis_index("sec") % 2
    core_id = core.reshape(1).astype(jnp.int32)
    term = lax.axis_index("term")
    factor = 1.0 / (blocks * sec * states * states)
    position = jnp.arange(states, dtype=jnp.int32)
    live_rows = position[None, :, None] < block_dims[:, None, None]
    live_cols = position[None, None, :] < block_dims[:, None, None]
    mask = live_rows & live_cols
    shape = jax.ShapeDtypeStruct

    core_pairs = [(i, i ^ 1) for i in range(sec)]
    chip_pairs = [(i, i + 1) for i in range(1, sec - 1, 2)]
    chip_pairs = chip_pairs + [(j, i) for i, j in chip_pairs]

    def swap(inner, outer):
        outer = lax.ppermute(outer, "sec", chip_pairs)
        inner = lax.ppermute(inner, "sec", core_pairs)
        return inner, outer

    def edges(x, axis):
        inner = lax.dynamic_index_in_dim(x, 1 - core, axis, keepdims=True)
        outer = lax.dynamic_index_in_dim(x, core, axis, keepdims=True)
        return inner, outer

    def rows(x, axis):
        return lax.dynamic_slice_in_dim(x, term * share, share, axis)

    at = jnp.arange(blocks, dtype=jnp.int32)[None, :] + term_shift[:, None]
    slot = jnp.where(at < 0, 3 - core, jnp.where(at > 1, 2 + core, at)).astype(jnp.int32)

    def apply_op(x, fields=(), paired=(), keep=True):
        outs = []
        if not fields:
            outs = [shape((groups, vecs, blocks, share, states), BF)]
        elif keep:
            outs = [shape((vecs, blocks, states, states), BF)]
        count = (len(fields), len(paired))
        if sum(count):
            outs.append(shape((sum(count), vecs, 8, 128), F32))
        result = call(
            functools.partial(apply_kernel, count),
            outs,
            [slot, x, right_all, left_env, *fields, *paired],
            smem=1,
            scratch=[pltpu.VMEM((blocks, left_env.shape[0] * states, vecs * states), BF)],
            flops=16 * vecs * blocks * states**3,
        )
        return result[0] if len(outs) == 1 else result

    def exchange(parts, axis="term"):
        return lax.all_to_all(parts, axis, 0, 0)

    barrier = lax.optimization_barrier

    slice_shape = shape((vecs, blocks, share, states), F32)
    edge_shape = shape((vecs, states, states), BF)
    four_shape = shape((vecs, 4, states, states), BF)
    lines = vecs * blocks * share

    right_all = jnp.concatenate([right_env, *swap(*edges(right_env, 1))], axis=1)
    start = jnp.where(mask[None], start_vectors, jnp.zeros((), BF))
    start_all = jnp.concatenate([start, *swap(*edges(start, 1))], axis=1)
    pre_core, pre_chip = swap(*edges(precond, 0))
    early = (rows(mask.astype(F32), 1), rows(precond, 1), rows(start, 2))
    start_all, early = barrier((start_all, early))
    mask_rows, pre, vec = early
    parts, pre_core, pre_chip = barrier((apply_op(start_all), pre_core, pre_chip))
    got = exchange(parts)
    h_raw, body = call(
        functools.partial(settle_kernel, factor),
        [slice_shape, shape((groups, lines + EXTRA, states), BF)],
        [got, mask_rows, vec, pre],
    )
    got = exchange(body)
    inner, outer, row = call(
        unpack_kernel, [edge_shape, edge_shape, shape((sec, 8, 128), F32)], [core_id, got], smem=1
    )
    h_core, h_chip = swap(inner, outer)
    row = exchange(row, "sec")
    dir_all, m_dir, coef = call(
        form_kernel,
        [four_shape, four_shape, shape((6, 8, 128), F32)],
        [row, got, h_core, h_chip, start_all, precond, pre_core, pre_chip],
    )
    parts, dir_all, m_dir = barrier((apply_op(dir_all), dir_all, m_dir))
    got = exchange(parts)
    h_dir, body = call(
        functools.partial(settle_kernel, factor),
        [slice_shape, shape((groups, lines, states), BF)],
        [got, mask_rows],
    )
    got = exchange(body)
    got, h_dir, m_dir, start_all = barrier((got, h_dir, m_dir, start_all))
    inner, outer = call(unpack_kernel, [edge_shape, edge_shape], [core_id, got], smem=1)
    hd_core, hd_chip = swap(inner, outer)
    (m_start,) = call(lift_start_kernel, [four_shape], [start_all, precond, pre_core, pre_chip])
    known = [m_start, m_dir, dir_all, start_all]
    h_m_start, dots_start = apply_op(m_start, known)
    h_m_dir, dots_dir = apply_op(m_dir, known)
    gram, direction = call(
        gram_kernel,
        [shape((len(PLAIN) + 2 * len(PAIRS), vecs, 8, 128), F32), slice_shape],
        [coef, vec, h_raw, h_dir, pre],
    )
    (m_hd,) = call(lift_kernel, [four_shape], [got, hd_core, hd_chip, precond, pre_core, pre_chip])
    dots_hd = apply_op(m_hd, [m_hd] + known, [h_m_start, h_m_dir], keep=False)
    everyone = groups * sec
    (row,) = call(
        functools.partial(tally_kernel, factor),
        [shape((everyone, 1, 128), F32)],
        [gram, dots_hd, dots_start, dots_dir],
    )
    row = exchange(row, ("term", "sec"))
    final, energy = call(
        finish_kernel,
        [slice_shape, shape((vecs,), F32)],
        [row, coef, vec, direction, h_raw, h_dir, pre],
        smem_outs=1,
    )
    return (final, energy)


def solution(mesh):
    return jax.shard_map(
        shards,
        mesh=mesh,
        in_specs=(
            P(None, "sec", None, None),
            P("term", "sec", None, None),
            P("term", "sec", None, None),
            P("term"),
            P("sec", None, None),
            P("sec"),
        ),
        out_specs=(P(None, "sec", "term", None), P()),
        check_vma=False,
    )
```

```python
import functools

import jax
import jax.numpy as jnp
from jax import lax
from jax.experimental import pallas as pl
from jax.experimental.pallas import tpu as pltpu
from jax.sharding import PartitionSpec as P


BF = jnp.bfloat16
F32 = jnp.float32
PAIRS = [(i, j) for i in range(4) for j in range(i, 4)]
PLAIN = [(0, 0), (0, 1), (1, 1), (0, 2), (0, 3), (1, 2), (1, 3)]
EXTRA = 16


def fold(product):
    rows, cols = product.shape
    tile = jnp.sum(product.reshape(rows // 8, 8, cols), axis=0)
    return sum(tile[:, i : i + 128] for i in range(0, cols, 128))


def slot_of(core_ref, shift_ref, k, b):
    at, core = b + shift_ref[k], core_ref[0]
    return jnp.where(at < 0, 3 - core, jnp.where(at > 1, 2 + core, at))


def apply_kernel(count, core_ref, shift_ref, x_ref, right_ref, left_ref, *refs):
    field_refs, paired_refs, rest = refs[: count[0]], refs[count[0] : sum(count)], refs[sum(count) :]
    out_ref, z_ref = rest[0], rest[-1]
    vecs, _, states, _ = x_ref.shape
    terms, blocks = left_ref.shape[:2]
    for k in range(terms):
        for b in range(blocks):
            slot = slot_of(core_ref, shift_ref, k, b)
            x = x_ref[:, slot].reshape(vecs * states, states)
            z = lax.dot_general(
                x, right_ref[k, slot], (((1,), (1,)), ((), ())), preferred_element_type=F32
            ).astype(BF)
            for u in range(vecs):
                z_ref[b, pl.ds(k * states, states), pl.ds(u * states, states)] = z[
                    u * states : (u + 1) * states
                ]
    if sum(count):
        dot_ref = rest[-2]
        dot_ref[...] = jnp.zeros_like(dot_ref)
    for b in range(blocks):
        wide = jnp.concatenate([left_ref[k, b] for k in range(terms)], axis=1)
        acc = jnp.dot(wide, z_ref[b], preferred_element_type=F32)
        for u in range(vecs):
            part = acc[:, u * states : (u + 1) * states]
            if not sum(count):
                groups, share = out_ref.shape[0], out_ref.shape[3]
                out_ref[:, u, b] = part.reshape(groups, share, states).astype(out_ref.dtype)
            elif len(rest) == 3:
                out_ref[u, b] = part.astype(out_ref.dtype)
            products = [part * f[u, b].astype(F32) for f in field_refs]
            products += [x_ref[u, b].astype(F32) * f[u, b].astype(F32) for f in paired_refs]
            for i, product in enumerate(products):
                dot_ref[i, u] = dot_ref[i, u] + fold(product)


def settle_kernel(factor, got_ref, mask_ref, *refs):
    h_ref, body_ref = refs[-2:]
    groups, vecs, blocks, share, states = got_ref.shape
    row = jnp.zeros((1, 128), F32)
    lane = lax.broadcasted_iota(jnp.int32, (1, 128), 1)
    for u in range(vecs):
        tiles = [jnp.zeros((8, 128), F32) for _ in range(8)]
        for b in range(blocks):
            h = got_ref[0, u, b].astype(F32)
            for t in range(1, groups):
                h = h + got_ref[t, u, b].astype(F32)
            h = h * mask_ref[b]
            h_ref[u, b] = h
            small = h.astype(BF)
            for t in range(groups):
                body_ref[t, pl.ds((u * blocks + b) * share, share), :] = small
            if len(refs) == 4:
                v, m = refs[0][u, b].astype(F32), refs[1][b]
                mv, mh = m * v, m * h
                products = [v * v, v * h, v * mv, v * mh, h * mh, mv * mv, mv * mh, mh * mh]
                tiles = [x + fold(y) for x, y in zip(tiles, products)]
        if len(refs) == 4:
            for i, tile in enumerate(tiles):
                row = row + jnp.where(lane == i * vecs + u, jnp.sum(tile) * factor, 0.0)
    if len(refs) == 4:
        high = row.astype(BF).astype(F32)
        middle = (row - high).astype(BF).astype(F32)
        low = row - high - middle
        index = lax.broadcasted_iota(jnp.int32, (EXTRA, 128), 0)
        tile = jnp.where(index == 0, high, jnp.where(index == 1, middle, jnp.where(index == 2, low, 0.0)))
        tile = tile.astype(BF)
        for t in range(groups):
            body_ref[t, pl.ds(vecs * blocks * share, EXTRA), pl.ds(0, 128)] = tile
            body_ref[t, pl.ds(vecs * blocks * share, EXTRA), pl.ds(128, states - 128)] = jnp.zeros(
                (EXTRA, states - 128), BF
            )


def block_of(got_ref, u, b, blocks, share):
    groups, _, states = got_ref.shape
    start = (u * blocks + b) * share
    if not isinstance(start, int):
        start = pl.multiple_of(start, share)
    return got_ref[:, pl.ds(start, share), :].reshape(groups * share, states)


def unpack_kernel(core_ref, got_ref, inner_ref, outer_ref, *row_refs):
    groups = got_ref.shape[0]
    vecs, states, _ = inner_ref.shape
    share = states // groups
    core = core_ref[0]
    for u in range(vecs):
        inner_ref[u] = block_of(got_ref, u, 1 - core, 2, share)
        outer_ref[u] = block_of(got_ref, u, core, 2, share)
    for row_ref in row_refs:
        tile = jnp.zeros((EXTRA, 128), F32)
        for t in range(groups):
            tile = tile + got_ref[t, pl.ds(vecs * states * 2 // groups, EXTRA), pl.ds(0, 128)].astype(F32)
        row_ref[...] = jnp.broadcast_to(jnp.sum(tile, axis=0, keepdims=True)[None], row_ref.shape)


def slot_blocks(own_ref, core_ref, chip_ref, u, share):
    own = [block_of(own_ref, u, b, 2, share) for b in range(2)]
    return own + [core_ref[u], chip_ref[u]]


def pick(row, i, vecs):
    return row if i == 0 else pltpu.roll(row, 128 - i * vecs, 1)


def lane_of(row, u):
    lane = lax.broadcasted_iota(jnp.int32, row.shape, 1)
    return jnp.sum(jnp.where(lane == u, row, 0.0), axis=1, keepdims=True)


def weight_of(own_ref, core_ref, chip_ref, i):
    if i < 2:
        return own_ref[i]
    ref = (core_ref, chip_ref)[i - 2]
    return ref[ref.shape[0] - 1].astype(F32)


def form_kernel(row_ref, got_ref, core_ref, chip_ref, start_ref, pre_ref, pre_core, pre_chip, dir_ref, mdir_ref, coef_ref):
    vecs, slots, states, _ = dir_ref.shape
    share = states // got_ref.shape[0]
    row = row_ref[0]
    for i in range(1, row_ref.shape[0]):
        row = row + row_ref[i]
    total = [pick(row, i, vecs) for i in range(8)]
    scale = 1.0 / jnp.sqrt(total[0] + 1e-06)
    vv, vh, vmv, vmh, hmh, mvmv, mvmh, mhmh = [x * (scale * scale) for x in total]
    correlation = vmh - vh * vmv
    square = mhmh - 2.0 * vh * mvmh + vh * vh * mvmv
    square = square - 2.0 * correlation * (vmh - vh * vmv) + correlation * correlation * vv
    norm = jnp.sqrt(jnp.maximum(square, 0.0) + 1e-06)
    coupling = (hmh - vh * vmh - correlation * vh) / norm
    alpha = scale / norm
    for j, x in enumerate([vh, correlation, alpha, scale, coupling, norm]):
        coef_ref[j] = jnp.broadcast_to(x, coef_ref.shape[1:])
    for u in range(vecs):
        ray, corr, mult = [lane_of(x[0:1], u) for x in (vh, correlation, alpha)]
        hs = slot_blocks(got_ref, core_ref, chip_ref, u, share)
        for i in range(slots):
            m = weight_of(pre_ref, pre_core, pre_chip, i)
            v = start_ref[u, i].astype(F32)
            raw = m * (hs[i].astype(F32) - ray * v) - corr * v
            small = (raw * mult).astype(BF)
            dir_ref[u, i] = small
            mdir_ref[u, i] = (m * small.astype(F32)).astype(BF)


def lift_kernel(got_ref, core_ref, chip_ref, pre_ref, pre_core, pre_chip, out_ref):
    vecs, slots, states, _ = out_ref.shape
    share = states // got_ref.shape[0]
    for u in range(vecs):
        hs = slot_blocks(got_ref, core_ref, chip_ref, u, share)
        for i in range(slots):
            m = weight_of(pre_ref, pre_core, pre_chip, i)
            out_ref[u, i] = (m * hs[i].astype(F32)).astype(BF)


def lift_start_kernel(start_ref, pre_ref, pre_core, pre_chip, out_ref):
    vecs, slots = out_ref.shape[:2]
    for u in range(vecs):
        for i in range(slots):
            m = weight_of(pre_ref, pre_core, pre_chip, i)
            out_ref[u, i] = (m * start_ref[u, i].astype(F32)).astype(BF)


def gram_kernel(coef_ref, start_ref, h_ref, hd_ref, pre_ref, dot_ref, dir_ref):
    vecs, blocks = h_ref.shape[:2]
    for u in range(vecs):
        rayleigh, correlation, alpha, scale = [lane_of(coef_ref[j, 0:1], u) for j in range(4)]
        for b in range(blocks):
            m = pre_ref[b]
            v, h = start_ref[u, b].astype(F32), h_ref[u, b]
            d = (m * (h - rayleigh * v) - correlation * v) * alpha
            dir_ref[u, b] = d
            basis = [v * scale, d, h * scale, hd_ref[u, b]]
            lifted = [m * x for x in basis]
            products = [basis[i] * basis[j] for i, j in PLAIN]
            products += [basis[i] * lifted[j] for i, j in PAIRS]
            products += [lifted[i] * lifted[j] for i, j in PAIRS]
            for i, product in enumerate(products):
                tile = fold(product)
                dot_ref[i, u] = tile if b == 0 else dot_ref[i, u] + tile


def tally_kernel(factor, *refs):
    out_ref = refs[-1]
    lines = []
    for ref in refs[:-1]:
        for i in range(ref.shape[0]):
            lines += [jnp.sum(ref[i, u], axis=0, keepdims=True) for u in range(ref.shape[1])]
    lines.append(jnp.zeros((128 - len(lines), 128), F32))
    table = jnp.concatenate(lines, axis=0)
    row = lax.dot_general(
        jnp.ones((8, 128), F32),
        table,
        (((1,), (1,)), ((), ())),
        precision=lax.Precision.HIGHEST,
        preferred_element_type=F32,
    )
    out_ref[...] = jnp.broadcast_to((row[0:1] * factor)[None], out_ref.shape)


def pack_kernel(core_ref, dims_hbm, start_ref, right_ref, pre_ref, out_ref, dims_ref, raw, weights, sem):
    terms, vecs = right_ref.shape[0], start_ref.shape[0]
    states = out_ref.shape[1]
    b = core_ref[0]
    copies = [pltpu.make_async_copy(dims_hbm, dims_ref, sem.at[0])]
    copies += [pltpu.make_async_copy(start_ref.at[u, b], raw.at[u], sem.at[1 + u]) for u in range(vecs)]
    copies.append(pltpu.make_async_copy(pre_ref.at[b], weights, sem.at[1 + vecs]))
    for k in range(terms):
        copies.append(pltpu.make_async_copy(right_ref.at[k, b], out_ref.at[k], sem.at[2 + vecs + k]))
    for copy in copies:
        copy.start()
    for copy in copies[: vecs + 2]:
        copy.wait()
    row = lax.broadcasted_iota(jnp.int32, (states, states), 0)
    col = lax.broadcasted_iota(jnp.int32, (states, states), 1)
    keep = (row < dims_ref[b]) & (col < dims_ref[b])
    for u in range(vecs):
        out_ref[terms + u] = jnp.where(keep, raw[u].astype(F32), 0.0).astype(BF)
    out_ref[terms + vecs] = weights[...].astype(BF)
    for copy in copies[vecs + 2 :]:
        copy.wait()


def load_kernel(core_ref, term_ref, dims_ref, start_ref, left_ref, right_ref, pre_ref, own_ref, left_out, right_out, mask_out, pre_out, vec_out, near_out, raw, weights, sem):
    vecs, blocks, states, _ = own_ref.shape
    terms = left_ref.shape[0]
    share = vec_out.shape[2]
    core = core_ref[0]
    first = pltpu.make_async_copy(start_ref, raw, sem.at[0])
    second = pltpu.make_async_copy(pre_ref, weights, sem.at[1])
    rest = []
    for k in range(terms):
        rest.append(pltpu.make_async_copy(right_ref.at[k, 1 - core], near_out.at[k], sem.at[2 + 3 * k]))
        rest.append(pltpu.make_async_copy(right_ref.at[k], right_out.at[k], sem.at[3 + 3 * k]))
        rest.append(pltpu.make_async_copy(left_ref.at[k], left_out.at[k], sem.at[4 + 3 * k]))
    for copy in [first, second] + rest:
        copy.start()
    here = pl.ds(pl.multiple_of(term_ref[0] * share, share), share)
    row = lax.broadcasted_iota(jnp.int32, (states, states), 0)
    col = lax.broadcasted_iota(jnp.int32, (states, states), 1)
    first.wait()
    for b in range(blocks):
        keep = (row < dims_ref[b]) & (col < dims_ref[b])
        for u in range(vecs):
            own_ref[u, b] = jnp.where(keep, raw[u, b].astype(F32), 0.0).astype(BF)
            vec_out[u, b] = own_ref[u, b, here, :]
        low = row[:share] + term_ref[0] * share
        mask_out[b] = jnp.where((low < dims_ref[b]) & (col[:share] < dims_ref[b]), 1.0, 0.0)
    second.wait()
    for b in range(blocks):
        pre_out[b] = weights[b, here, :]
    for u in range(vecs):
        near_out[terms + u] = own_ref[u, 1 - core]
    near_out[terms + vecs] = weights[1 - core].astype(BF)
    for copy in rest:
        copy.wait()


def form(table, left, right):
    result = None
    for i, x in left:
        for j, y in right:
            term = x * y * table[(min(i, j), max(i, j))]
            result = term if result is None else result + term
    return result


def lowest(rayleigh, curvature, coupling):
    half = 0.5 * (rayleigh - curvature)
    energy = 0.5 * (rayleigh + curvature) - jnp.sqrt(half * half + coupling * coupling)
    weight = energy - rayleigh
    return energy, weight, jnp.sqrt(coupling * coupling + weight * weight)


def finish_kernel(row_ref, coef_ref, start_ref, dir_ref, h_ref, hd_ref, pre_ref, out_ref, energy_ref):
    vecs, blocks = out_ref.shape[:2]
    row = row_ref[0]
    for i in range(1, row_ref.shape[0]):
        row = row + row_ref[i]
    count = len(PLAIN) + 2 * len(PAIRS) + 15
    total = [pick(row, i, vecs) for i in range(count)]
    one = {p: total[i] for i, p in enumerate(PLAIN)}
    first = {p: total[len(PLAIN) + i] for i, p in enumerate(PAIRS)}
    second = {p: total[len(PLAIN) + len(PAIRS) + i] for i, p in enumerate(PAIRS)}
    far = total[len(PLAIN) + 2 * len(PAIRS) :]
    old_ray, old_corr, _, scale, coupling, old_norm = [coef_ref[j, 0:1] for j in range(6)]

    _, weight, size = lowest(old_ray, one[(1, 3)], coupling)
    keep, mix = coupling / size, weight / size
    v_of, h_of = [(0, keep), (1, mix)], [(2, keep), (3, mix)]
    rayleigh = form(one, v_of, h_of)
    resid_of = h_of + [(i, -rayleigh * x) for i, x in v_of]
    correlation = form(first, v_of, resid_of)
    square = form(second, resid_of, resid_of) - 2.0 * correlation * form(first, v_of, resid_of)
    square = square + correlation * correlation * form(one, v_of, v_of)
    norm = jnp.sqrt(jnp.maximum(square, 0.0) + 1e-06)
    coupling = (form(first, resid_of, h_of) - correlation * rayleigh) / norm

    mult = [
        mix,
        scale * keep * (old_ray - rayleigh),
        -rayleigh * mix,
        keep * old_norm - correlation * mix,
        scale * keep * (old_corr - correlation),
    ]
    back = 1.0 / scale
    on_hd = far[:5]
    on_start = [far[5]] + [far[7 + i] for i in range(4)]
    on_dir = [far[6]] + [far[11 + i] for i in range(4)]
    on_d = [first[3, 3], first[0, 3] * back, first[1, 3], one[1, 3], one[0, 3] * back]
    on_v = [first[2, 3], first[0, 2] * back, first[1, 2], one[1, 2], one[0, 2] * back]
    curvature = None
    for j, column in enumerate([on_hd, on_start, on_dir, on_d, on_v]):
        line = None
        for i in range(5):
            term = mult[i] * column[i]
            line = term if line is None else line + term
        line = line * (mult[j] * back if j == 4 else mult[j])
        curvature = line if curvature is None else curvature + line
    curvature = curvature / (norm * norm)
    energy, weight, size = lowest(rayleigh, curvature, coupling)
    of_v, of_raw = coupling / size, weight / (norm * size)
    values = (keep * scale, mix, rayleigh, correlation, of_v, of_raw)
    for u in range(vecs):
        energy_ref[u] = lane_of(energy, u)[0, 0]
        first_v, then_d, ray, corr, use_v, use_raw = [lane_of(x, u) for x in values]
        for b in range(blocks):
            new_v = first_v * start_ref[u, b].astype(F32) + then_d * dir_ref[u, b]
            new_h = first_v * h_ref[u, b] + then_d * hd_ref[u, b]
            raw = pre_ref[b] * (new_h - ray * new_v) - corr * new_v
            out_ref[u, b] = use_v * new_v + use_raw * raw


def call(kernel, outs, args, smem=0, scratch=(), flops=0, smem_outs=0, anywhere=False):
    vmem = pl.BlockSpec(memory_space=pltpu.VMEM)
    bulk = pl.BlockSpec(memory_space=pltpu.HBM) if anywhere else vmem
    specs = [pl.BlockSpec(memory_space=pltpu.SMEM)] * smem + [bulk] * (len(args) - smem)
    size = sum(x.size * x.dtype.itemsize for x in list(outs) + list(args))
    return pl.pallas_call(
        kernel,
        out_shape=[jax.ShapeDtypeStruct(x.shape, x.dtype) for x in outs],
        in_specs=specs,
        out_specs=[vmem] * (len(outs) - smem_outs)
        + [pl.BlockSpec(memory_space=pltpu.SMEM)] * smem_outs,
        scratch_shapes=scratch,
        compiler_params=pltpu.CompilerParams(vmem_limit_bytes=24 << 20),
        cost_estimate=pl.CostEstimate(flops=flops, bytes_accessed=size, transcendentals=0),
    )(*args)


def shards(start_vectors, left_env, right_env, term_shift, precond, block_dims):
    vecs, blocks, states, _ = start_vectors.shape
    groups = lax.axis_size("term")
    sec = lax.axis_size("sec")
    share = states // groups
    core_id = (lax.axis_index("sec") & 1).reshape(1)
    term_id = lax.axis_index("term").reshape(1)
    factor = 1.0 / (blocks * sec * states * states)
    shape = jax.ShapeDtypeStruct

    core_pairs = [(i, i ^ 1) for i in range(sec)]
    chip_pairs = [(i, i + 1) for i in range(1, sec - 1, 2)]
    chip_pairs = chip_pairs + [(j, i) for i, j in chip_pairs]

    def far(x):
        return lax.ppermute(x, "sec", chip_pairs)

    def near(x):
        return lax.ppermute(x, "sec", core_pairs)

    def apply_op(x, fields=(), paired=(), keep=True):
        outs = []
        if not fields:
            outs = [shape((groups, vecs, blocks, share, states), BF)]
        elif keep:
            outs = [shape((vecs, blocks, states, states), BF)]
        count = (len(fields), len(paired))
        if sum(count):
            outs.append(shape((sum(count), vecs, 8, 128), F32))
        result = call(
            functools.partial(apply_kernel, count),
            outs,
            [core_id, term_shift, x, right_all, left_here, *fields, *paired],
            smem=2,
            scratch=[pltpu.VMEM((blocks, left_env.shape[0] * states, vecs * states), BF)],
            flops=16 * vecs * blocks * states**3,
        )
        return result[0] if len(outs) == 1 else result

    def exchange(parts, axis="term"):
        return lax.all_to_all(parts, axis, 0, 0)

    barrier = lax.optimization_barrier

    slice_shape = shape((vecs, blocks, share, states), F32)
    edge_shape = shape((vecs, states, states), BF)
    four_shape = shape((vecs, 4, states, states), BF)
    lines = vecs * blocks * share
    terms = right_env.shape[0]

    def in_hbm(x):
        return pltpu.with_memory_space_constraint(x, pltpu.HBM)

    start_hbm, left_hbm, right_hbm, pre_hbm = [
        in_hbm(x) for x in (start_vectors, left_env, right_env, precond)
    ]

    (pack_chip,) = call(
        pack_kernel,
        [shape((terms + vecs + 1, states, states), BF)],
        [core_id, in_hbm(block_dims), start_hbm, right_hbm, pre_hbm],
        smem=1,
        scratch=[
            pltpu.SMEM(block_dims.shape, jnp.int32),
            pltpu.VMEM((vecs, states, states), BF),
            pltpu.VMEM((states, states), F32),
            pltpu.SemaphoreType.DMA((2 + vecs + terms,)),
        ],
        anywhere=True,
    )
    pack_chip = far(pack_chip)
    start, left_here, right_here, mask_rows, pre, vec, pack_core = call(
        load_kernel,
        [
            shape(start_vectors.shape, BF),
            shape(left_env.shape, BF),
            shape(right_env.shape, BF),
            shape((blocks, share, states), F32),
            shape((blocks, share, states), F32),
            shape((vecs, blocks, share, states), BF),
            shape((terms + vecs + 1, states, states), BF),
        ],
        [core_id, term_id, block_dims, start_hbm, left_hbm, right_hbm, pre_hbm],
        smem=3,
        scratch=[
            pltpu.VMEM(start_vectors.shape, BF),
            pltpu.VMEM(precond.shape, F32),
            pltpu.SemaphoreType.DMA((2 + 3 * terms,)),
        ],
        anywhere=True,
    )
    pack_core = near(pack_core)
    packs = [pack_core, pack_chip]
    right_all = jnp.concatenate([right_here] + [x[:terms, None] for x in packs], axis=1)
    start_all = jnp.concatenate([start] + [x[terms : terms + vecs, None] for x in packs], axis=1)
    got = exchange(apply_op(start_all))
    h_raw, body = call(
        functools.partial(settle_kernel, factor),
        [slice_shape, shape((groups, lines + EXTRA, states), BF)],
        [got, mask_rows, vec, pre],
    )
    got = exchange(body)
    inner, outer, row = call(
        unpack_kernel, [edge_shape, edge_shape, shape((sec, 1, 128), F32)], [core_id, got], smem=1
    )
    h_chip, h_core = far(outer), near(inner)
    row = exchange(row, "sec")
    dir_all, m_dir, coef = call(
        form_kernel,
        [four_shape, four_shape, shape((6, 8, 128), F32)],
        [row, got, h_core, h_chip, start_all, precond, *packs],
    )
    parts, dir_all, m_dir = barrier((apply_op(dir_all), dir_all, m_dir))
    got = exchange(parts)
    h_dir, body = call(
        functools.partial(settle_kernel, factor),
        [slice_shape, shape((groups, lines, states), BF)],
        [got, mask_rows],
    )
    got = exchange(body)
    got, h_dir, m_dir, start_all = barrier((got, h_dir, m_dir, start_all))
    inner, outer = call(unpack_kernel, [edge_shape, edge_shape], [core_id, got], smem=1)
    hd_chip, hd_core = far(outer), near(inner)
    (m_start,) = call(lift_start_kernel, [four_shape], [start_all, precond, *packs])
    known = [m_start, m_dir, dir_all, start_all]
    h_m_start, dots_start = apply_op(m_start, known)
    h_m_dir, dots_dir = apply_op(m_dir, known)
    gram, direction = call(
        gram_kernel,
        [shape((len(PLAIN) + 2 * len(PAIRS), vecs, 8, 128), F32), slice_shape],
        [coef, vec, h_raw, h_dir, pre],
    )
    (m_hd,) = call(lift_kernel, [four_shape], [got, hd_core, hd_chip, precond, *packs])
    dots_hd = apply_op(m_hd, [m_hd] + known, [h_m_start, h_m_dir], keep=False)
    everyone = groups * sec
    (row,) = call(
        functools.partial(tally_kernel, factor),
        [shape((everyone, 1, 128), F32)],
        [gram, dots_hd, dots_start, dots_dir],
    )
    row = exchange(row, ("term", "sec"))
    final, energy = call(
        finish_kernel,
        [slice_shape, shape((vecs,), F32)],
        [row, coef, vec, direction, h_raw, h_dir, pre],
        smem_outs=1,
    )
    return (final, energy)


def solution(mesh):
    return jax.shard_map(
        shards,
        mesh=mesh,
        in_specs=(
            P(None, "sec", None, None),
            P("term", "sec", None, None),
            P("term", "sec", None, None),
            P("term"),
            P("sec", None, None),
            P("sec"),
        ),
        out_specs=(P(None, "sec", "term", None), P()),
        check_vma=False,
    )
```

```python
import functools

import jax
import jax.numpy as jnp
from jax import lax
from jax.experimental import pallas as pl
from jax.experimental.pallas import tpu as pltpu
from jax.sharding import PartitionSpec as P


BF = jnp.bfloat16
F32 = jnp.float32
PAIRS = [(i, j) for i in range(4) for j in range(i, 4)]
PLAIN = [(0, 0), (0, 1), (1, 1), (0, 2), (0, 3), (1, 2), (1, 3)]
EXTRA = 8


def fold(product):
    rows, cols = product.shape
    tile = jnp.sum(product.reshape(rows // 8, 8, cols), axis=0)
    return sum(tile[:, i : i + 128] for i in range(0, cols, 128))


def slot_of(core_ref, shift_ref, k, b):
    at, core = b + shift_ref[k], core_ref[0]
    return jnp.where(at < 0, 3 - core, jnp.where(at > 1, 2 + core, at))


def apply_kernel(count, core_ref, shift_ref, x_ref, right_ref, left_ref, *refs):
    field_refs, paired_refs, rest = refs[: count[0]], refs[count[0] : sum(count)], refs[sum(count) :]
    out_ref, z_ref = rest[0], rest[-1]
    vecs, _, states, _ = x_ref.shape
    terms, blocks = left_ref.shape[:2]
    for k in range(terms):
        for b in range(blocks):
            slot = slot_of(core_ref, shift_ref, k, b)
            x = x_ref[:, slot].reshape(vecs * states, states)
            z = lax.dot_general(
                x, right_ref[k, slot], (((1,), (1,)), ((), ())), preferred_element_type=F32
            ).astype(BF)
            for u in range(vecs):
                z_ref[b, pl.ds(k * states, states), pl.ds(u * states, states)] = z[
                    u * states : (u + 1) * states
                ]
    if sum(count):
        dot_ref = rest[-2]
        dot_ref[...] = jnp.zeros_like(dot_ref)
    for b in range(blocks):
        wide = jnp.concatenate([left_ref[k, b] for k in range(terms)], axis=1)
        acc = jnp.dot(wide, z_ref[b], preferred_element_type=F32)
        for u in range(vecs):
            part = acc[:, u * states : (u + 1) * states]
            if not sum(count):
                groups, share = out_ref.shape[0], out_ref.shape[3]
                out_ref[:, u, b] = part.reshape(groups, share, states).astype(out_ref.dtype)
            elif len(rest) == 3:
                out_ref[u, b] = part.astype(out_ref.dtype)
            products = [part * f[u, b].astype(F32) for f in field_refs]
            products += [x_ref[u, b].astype(F32) * f[u, b].astype(F32) for f in paired_refs]
            for i, product in enumerate(products):
                dot_ref[i, u] = dot_ref[i, u] + fold(product)


def settle_kernel(factor, got_ref, mask_ref, *refs):
    h_ref, body_ref = refs[-2:]
    groups, vecs, blocks, share, states = got_ref.shape
    row = jnp.zeros((1, 128), F32)
    lane = lax.broadcasted_iota(jnp.int32, (1, 128), 1)
    for u in range(vecs):
        tiles = [jnp.zeros((8, 128), F32) for _ in range(8)]
        for b in range(blocks):
            h = got_ref[0, u, b].astype(F32)
            for t in range(1, groups):
                h = h + got_ref[t, u, b].astype(F32)
            h = h * mask_ref[b]
            h_ref[u, b] = h
            small = h.astype(BF)
            for t in range(groups):
                body_ref[t, pl.ds((u * blocks + b) * share, share), :] = small
            if len(refs) == 4:
                v, m = refs[0][u, b].astype(F32), refs[1][b]
                mv, mh = m * v, m * h
                products = [v * v, v * h, v * mv, v * mh, h * mh, mv * mv, mv * mh, mh * mh]
                tiles = [x + fold(y) for x, y in zip(tiles, products)]
        if len(refs) == 4:
            for i, tile in enumerate(tiles):
                row = row + jnp.where(lane == i * vecs + u, jnp.sum(tile) * factor, 0.0)
    if len(refs) == 4:
        high = row.astype(BF).astype(F32)
        middle = (row - high).astype(BF).astype(F32)
        low = row - high - middle
        index = lax.broadcasted_iota(jnp.int32, (EXTRA, 128), 0)
        tile = jnp.where(index == 0, high, jnp.where(index == 1, middle, jnp.where(index == 2, low, 0.0)))
        tile = tile.astype(BF)
        for t in range(groups):
            body_ref[t, pl.ds(vecs * blocks * share, EXTRA), pl.ds(0, 128)] = tile
            body_ref[t, pl.ds(vecs * blocks * share, EXTRA), pl.ds(128, states - 128)] = jnp.zeros(
                (EXTRA, states - 128), BF
            )


def block_of(got_ref, u, b, blocks, share):
    groups, _, states = got_ref.shape
    start = (u * blocks + b) * share
    if not isinstance(start, int):
        start = pl.multiple_of(start, share)
    return got_ref[:, pl.ds(start, share), :].reshape(groups * share, states)


def unpack_kernel(core_ref, got_ref, *refs):
    inner_ref, outer_ref = refs[1:3] if len(refs) == 4 else refs
    groups, _, states = got_ref.shape
    vecs, share = 2, states // groups
    core = core_ref[0]
    for ref, b in ((inner_ref, 1 - core), (outer_ref, core)):
        for u in range(vecs):
            ref[u] = block_of(got_ref, u, b, 2, share)
        if len(refs) == 4:
            ref[vecs] = refs[0][b].astype(BF)
    if len(refs) == 4:
        tile = jnp.zeros((EXTRA, 128), F32)
        for t in range(groups):
            tile = tile + got_ref[t, pl.ds(vecs * 2 * share, EXTRA), pl.ds(0, 128)].astype(F32)
        row_ref = refs[3]
        row_ref[...] = jnp.broadcast_to(jnp.sum(tile, axis=0, keepdims=True)[None], row_ref.shape)


def slot_blocks(own_ref, core_ref, chip_ref, u, share):
    own = [block_of(own_ref, u, b, 2, share) for b in range(2)]
    return own + [core_ref[u], chip_ref[u]]


def pick(row, i, vecs):
    return row if i == 0 else pltpu.roll(row, 128 - i * vecs, 1)


def lane_of(row, u):
    lane = lax.broadcasted_iota(jnp.int32, row.shape, 1)
    return jnp.sum(jnp.where(lane == u, row, 0.0), axis=1, keepdims=True)


def weight_of(own_ref, core_ref, chip_ref, i):
    if i < 2:
        return own_ref[i]
    ref = (core_ref, chip_ref)[i - 2]
    return ref[ref.shape[0] - 1].astype(F32)


def form_kernel(row_ref, got_ref, core_ref, chip_ref, start_ref, pre_ref, pre_core, pre_chip, dir_ref, mdir_ref, coef_ref):
    vecs, slots, states, _ = dir_ref.shape
    share = states // got_ref.shape[0]
    row = row_ref[0]
    for i in range(1, row_ref.shape[0]):
        row = row + row_ref[i]
    total = [pick(row, i, vecs) for i in range(8)]
    scale = 1.0 / jnp.sqrt(total[0] + 1e-06)
    vv, vh, vmv, vmh, hmh, mvmv, mvmh, mhmh = [x * (scale * scale) for x in total]
    correlation = vmh - vh * vmv
    square = mhmh - 2.0 * vh * mvmh + vh * vh * mvmv
    square = square - 2.0 * correlation * (vmh - vh * vmv) + correlation * correlation * vv
    norm = jnp.sqrt(jnp.maximum(square, 0.0) + 1e-06)
    coupling = (hmh - vh * vmh - correlation * vh) / norm
    alpha = scale / norm
    for j, x in enumerate([vh, correlation, alpha, scale, coupling, norm]):
        coef_ref[j] = jnp.broadcast_to(x, coef_ref.shape[1:])
    for u in range(vecs):
        ray, corr, mult = [lane_of(x[0:1], u) for x in (vh, correlation, alpha)]
        hs = slot_blocks(got_ref, core_ref, chip_ref, u, share)
        for i in range(slots):
            m = weight_of(pre_ref, pre_core, pre_chip, i)
            v = start_ref[u, i].astype(F32)
            raw = m * (hs[i].astype(F32) - ray * v) - corr * v
            small = (raw * mult).astype(BF)
            dir_ref[u, i] = small
            mdir_ref[u, i] = (m * small.astype(F32)).astype(BF)


def lift_kernel(got_ref, core_ref, chip_ref, pre_ref, pre_core, pre_chip, out_ref):
    vecs, slots, states, _ = out_ref.shape
    share = states // got_ref.shape[0]
    for u in range(vecs):
        hs = slot_blocks(got_ref, core_ref, chip_ref, u, share)
        for i in range(slots):
            m = weight_of(pre_ref, pre_core, pre_chip, i)
            out_ref[u, i] = (m * hs[i].astype(F32)).astype(BF)


def lift_start_kernel(start_ref, pre_ref, pre_core, pre_chip, out_ref):
    vecs, slots = out_ref.shape[:2]
    for u in range(vecs):
        for i in range(slots):
            m = weight_of(pre_ref, pre_core, pre_chip, i)
            out_ref[u, i] = (m * start_ref[u, i].astype(F32)).astype(BF)


def gram_kernel(coef_ref, start_ref, h_ref, hd_ref, pre_ref, dot_ref, dir_ref):
    vecs, blocks = h_ref.shape[:2]
    for u in range(vecs):
        rayleigh, correlation, alpha, scale = [lane_of(coef_ref[j, 0:1], u) for j in range(4)]
        for b in range(blocks):
            m = pre_ref[b]
            v, h = start_ref[u, b].astype(F32), h_ref[u, b]
            d = (m * (h - rayleigh * v) - correlation * v) * alpha
            dir_ref[u, b] = d
            basis = [v * scale, d, h * scale, hd_ref[u, b]]
            lifted = [m * x for x in basis]
            products = [basis[i] * basis[j] for i, j in PLAIN]
            products += [basis[i] * lifted[j] for i, j in PAIRS]
            products += [lifted[i] * lifted[j] for i, j in PAIRS]
            for i, product in enumerate(products):
                tile = fold(product)
                dot_ref[i, u] = tile if b == 0 else dot_ref[i, u] + tile


def tally_kernel(factor, *refs):
    out_ref = refs[-1]
    lines = []
    for ref in refs[:-1]:
        for i in range(ref.shape[0]):
            lines += [jnp.sum(ref[i, u], axis=0, keepdims=True) for u in range(ref.shape[1])]
    lines.append(jnp.zeros((128 - len(lines), 128), F32))
    table = jnp.concatenate(lines, axis=0)
    row = lax.dot_general(
        jnp.ones((8, 128), F32),
        table,
        (((1,), (1,)), ((), ())),
        precision=lax.Precision.HIGHEST,
        preferred_element_type=F32,
    )
    out_ref[...] = jnp.broadcast_to((row[0:1] * factor)[None], out_ref.shape)


def pack_kernel(core_ref, dims_hbm, start_ref, right_ref, out_ref, dims_ref, raw, sem):
    terms, vecs = right_ref.shape[0], start_ref.shape[0]
    states = out_ref.shape[1]
    b = core_ref[0]
    copies = [pltpu.make_async_copy(dims_hbm, dims_ref, sem.at[0])]
    copies += [pltpu.make_async_copy(start_ref.at[u, b], raw.at[u], sem.at[1 + u]) for u in range(vecs)]
    for k in range(terms):
        copies.append(pltpu.make_async_copy(right_ref.at[k, b], out_ref.at[k], sem.at[1 + vecs + k]))
    for copy in copies:
        copy.start()
    for copy in copies[: vecs + 1]:
        copy.wait()
    row = lax.broadcasted_iota(jnp.int32, (states, states), 0)
    col = lax.broadcasted_iota(jnp.int32, (states, states), 1)
    keep = (row < dims_ref[b]) & (col < dims_ref[b])
    for u in range(vecs):
        out_ref[terms + u] = jnp.where(keep, raw[u].astype(F32), 0.0).astype(BF)
    for copy in copies[vecs + 1 :]:
        copy.wait()


def load_kernel(core_ref, term_ref, dims_ref, shift_ref, start_ref, left_ref, right_ref, pre_ref, own_ref, left_out, right_out, mask_out, pre_out, vec_out, near_out, raw, weights, sem):
    vecs, blocks, states, _ = own_ref.shape
    terms = left_ref.shape[0]
    share = vec_out.shape[2]
    core = core_ref[0]
    first = pltpu.make_async_copy(start_ref, raw, sem.at[0])
    second = pltpu.make_async_copy(pre_ref, weights, sem.at[1])
    rest = []
    for k in range(terms):
        rest.append(pltpu.make_async_copy(right_ref.at[k, 1 - core], near_out.at[k], sem.at[2 + 3 * k]))
        rest.append(pltpu.make_async_copy(right_ref.at[k], right_out.at[k], sem.at[3 + 3 * k]))
        rest.append(pltpu.make_async_copy(left_ref.at[k], left_out.at[k], sem.at[4 + 3 * k]))
    for copy in [first, second] + rest:
        copy.start()
    here = pl.ds(pl.multiple_of(term_ref[0] * share, share), share)
    row = lax.broadcasted_iota(jnp.int32, (states, states), 0)
    col = lax.broadcasted_iota(jnp.int32, (states, states), 1)
    first.wait()
    for b in range(blocks):
        keep = (row < dims_ref[b]) & (col < dims_ref[b])
        for u in range(vecs):
            own_ref[u, b] = jnp.where(keep, raw[u, b].astype(F32), 0.0).astype(BF)
            vec_out[u, b] = own_ref[u, b, here, :]
        low = row[:share] + term_ref[0] * share
        mask_out[b] = jnp.where((low < dims_ref[b]) & (col[:share] < dims_ref[b]), 1.0, 0.0)
    second.wait()
    for b in range(blocks):
        pre_out[b] = weights[b, here, :]
    for u in range(vecs):
        near_out[terms + u] = own_ref[u, 1 - core]
    for copy in rest:
        copy.wait()


def form(table, left, right):
    result = None
    for i, x in left:
        for j, y in right:
            term = x * y * table[(min(i, j), max(i, j))]
            result = term if result is None else result + term
    return result


def lowest(rayleigh, curvature, coupling):
    half = 0.5 * (rayleigh - curvature)
    energy = 0.5 * (rayleigh + curvature) - jnp.sqrt(half * half + coupling * coupling)
    weight = energy - rayleigh
    return energy, weight, jnp.sqrt(coupling * coupling + weight * weight)


def finish_kernel(row_ref, coef_ref, start_ref, dir_ref, h_ref, hd_ref, pre_ref, out_ref, energy_ref):
    vecs, blocks = out_ref.shape[:2]
    chains = [row_ref[i] for i in range(16)]
    for i in range(16, row_ref.shape[0]):
        chains[i % 16] = chains[i % 16] + row_ref[i]
    while len(chains) > 1:
        chains = [x + y for x, y in zip(chains[::2], chains[1::2])]
    row = chains[0]
    count = len(PLAIN) + 2 * len(PAIRS) + 15
    total = [pick(row, i, vecs) for i in range(count)]
    one = {p: total[i] for i, p in enumerate(PLAIN)}
    first = {p: total[len(PLAIN) + i] for i, p in enumerate(PAIRS)}
    second = {p: total[len(PLAIN) + len(PAIRS) + i] for i, p in enumerate(PAIRS)}
    far = total[len(PLAIN) + 2 * len(PAIRS) :]
    old_ray, old_corr, _, scale, coupling, old_norm = [coef_ref[j, 0:1] for j in range(6)]

    _, weight, size = lowest(old_ray, one[(1, 3)], coupling)
    keep, mix = coupling / size, weight / size
    v_of, h_of = [(0, keep), (1, mix)], [(2, keep), (3, mix)]
    rayleigh = form(one, v_of, h_of)
    resid_of = h_of + [(i, -rayleigh * x) for i, x in v_of]
    correlation = form(first, v_of, resid_of)
    square = form(second, resid_of, resid_of) - 2.0 * correlation * form(first, v_of, resid_of)
    square = square + correlation * correlation * form(one, v_of, v_of)
    norm = jnp.sqrt(jnp.maximum(square, 0.0) + 1e-06)
    coupling = (form(first, resid_of, h_of) - correlation * rayleigh) / norm

    mult = [
        mix,
        scale * keep * (old_ray - rayleigh),
        -rayleigh * mix,
        keep * old_norm - correlation * mix,
        scale * keep * (old_corr - correlation),
    ]
    back = 1.0 / scale
    on_hd = far[:5]
    on_start = [far[5]] + [far[7 + i] for i in range(4)]
    on_dir = [far[6]] + [far[11 + i] for i in range(4)]
    on_d = [first[3, 3], first[0, 3] * back, first[1, 3], one[1, 3], one[0, 3] * back]
    on_v = [first[2, 3], first[0, 2] * back, first[1, 2], one[1, 2], one[0, 2] * back]
    curvature = None
    for j, column in enumerate([on_hd, on_start, on_dir, on_d, on_v]):
        line = None
        for i in range(5):
            term = mult[i] * column[i]
            line = term if line is None else line + term
        line = line * (mult[j] * back if j == 4 else mult[j])
        curvature = line if curvature is None else curvature + line
    curvature = curvature / (norm * norm)
    energy, weight, size = lowest(rayleigh, curvature, coupling)
    of_v, of_raw = coupling / size, weight / (norm * size)
    values = (keep * scale, mix, rayleigh, correlation, of_v, of_raw)
    for u in range(vecs):
        energy_ref[u] = lane_of(energy, u)[0, 0]
        first_v, then_d, ray, corr, use_v, use_raw = [lane_of(x, u) for x in values]
        for b in range(blocks):
            new_v = first_v * start_ref[u, b].astype(F32) + then_d * dir_ref[u, b]
            new_h = first_v * h_ref[u, b] + then_d * hd_ref[u, b]
            raw = pre_ref[b] * (new_h - ray * new_v) - corr * new_v
            out_ref[u, b] = use_v * new_v + use_raw * raw


def call(kernel, outs, args, smem=0, scratch=(), flops=0, smem_outs=0, anywhere=False):
    vmem = pl.BlockSpec(memory_space=pltpu.VMEM)
    bulk = pl.BlockSpec(memory_space=pltpu.HBM) if anywhere else vmem
    specs = [pl.BlockSpec(memory_space=pltpu.SMEM)] * smem + [bulk] * (len(args) - smem)
    size = sum(x.size * x.dtype.itemsize for x in list(outs) + list(args))
    return pl.pallas_call(
        kernel,
        out_shape=[jax.ShapeDtypeStruct(x.shape, x.dtype) for x in outs],
        in_specs=specs,
        out_specs=[vmem] * (len(outs) - smem_outs)
        + [pl.BlockSpec(memory_space=pltpu.SMEM)] * smem_outs,
        scratch_shapes=scratch,
        compiler_params=pltpu.CompilerParams(vmem_limit_bytes=24 << 20),
        cost_estimate=pl.CostEstimate(flops=flops, bytes_accessed=size, transcendentals=0),
    )(*args)


def shards(start_vectors, left_env, right_env, term_shift, precond, block_dims):
    vecs, blocks, states, _ = start_vectors.shape
    groups = lax.axis_size("term")
    sec = lax.axis_size("sec")
    share = states // groups
    core_id = (lax.axis_index("sec") & 1).reshape(1)
    term_id = lax.axis_index("term").reshape(1)
    factor = 1.0 / (blocks * sec * states * states)
    shape = jax.ShapeDtypeStruct

    core_pairs = [(i, i ^ 1) for i in range(sec)]
    chip_pairs = [(i, i + 1) for i in range(1, sec - 1, 2)]
    chip_pairs = chip_pairs + [(j, i) for i, j in chip_pairs]

    def far(x):
        return lax.ppermute(x, "sec", chip_pairs)

    def near(x):
        return lax.ppermute(x, "sec", core_pairs)

    def apply_op(x, fields=(), paired=(), keep=True):
        outs = []
        if not fields:
            outs = [shape((groups, vecs, blocks, share, states), BF)]
        elif keep:
            outs = [shape((vecs, blocks, states, states), BF)]
        count = (len(fields), len(paired))
        if sum(count):
            outs.append(shape((sum(count), vecs, 8, 128), F32))
        result = call(
            functools.partial(apply_kernel, count),
            outs,
            [core_id, term_shift, x, right_all, left_here, *fields, *paired],
            smem=2,
            scratch=[pltpu.VMEM((blocks, left_env.shape[0] * states, vecs * states), BF)],
            flops=16 * vecs * blocks * states**3,
        )
        return result[0] if len(outs) == 1 else result

    def exchange(parts, axis="term"):
        return lax.all_to_all(parts, axis, 0, 0)

    barrier = lax.optimization_barrier

    slice_shape = shape((vecs, blocks, share, states), F32)
    edge_shape = shape((vecs, states, states), BF)
    four_shape = shape((vecs, 4, states, states), BF)
    lines = vecs * blocks * share
    terms = right_env.shape[0]

    def in_hbm(x):
        return pltpu.with_memory_space_constraint(x, pltpu.HBM)

    start_hbm, left_hbm, right_hbm, pre_hbm = [
        in_hbm(x) for x in (start_vectors, left_env, right_env, precond)
    ]

    (pack_chip,) = call(
        pack_kernel,
        [shape((terms + vecs, states, states), BF)],
        [core_id, in_hbm(block_dims), start_hbm, right_hbm],
        smem=1,
        scratch=[
            pltpu.SMEM(block_dims.shape, jnp.int32),
            pltpu.VMEM((vecs, states, states), BF),
            pltpu.SemaphoreType.DMA((1 + vecs + terms,)),
        ],
        anywhere=True,
    )
    pack_chip = far(pack_chip)
    start, left_here, right_here, mask_rows, pre, vec, pack_core = call(
        load_kernel,
        [
            shape(start_vectors.shape, BF),
            shape(left_env.shape, BF),
            shape(right_env.shape, BF),
            shape((blocks, share, states), F32),
            shape((blocks, share, states), F32),
            shape((vecs, blocks, share, states), BF),
            shape((terms + vecs, states, states), BF),
        ],
        [core_id, term_id, block_dims, term_shift, start_hbm, left_hbm, right_hbm, pre_hbm],
        smem=4,
        scratch=[
            pltpu.VMEM(start_vectors.shape, BF),
            pltpu.VMEM(precond.shape, F32),
            pltpu.SemaphoreType.DMA((2 + 3 * terms,)),
        ],
        anywhere=True,
    )
    pack_core = near(pack_core)
    packs = [pack_core, pack_chip]
    right_all = jnp.concatenate([right_here] + [x[:terms, None] for x in packs], axis=1)
    start_all = jnp.concatenate([start] + [x[terms:, None] for x in packs], axis=1)
    got = exchange(apply_op(start_all))
    h_raw, body = call(
        functools.partial(settle_kernel, factor),
        [slice_shape, shape((groups, lines + EXTRA, states), BF)],
        [got, mask_rows, vec, pre],
    )
    got = exchange(body)
    pack_shape = shape((vecs + 1, states, states), BF)
    inner, outer, row = call(
        unpack_kernel,
        [pack_shape, pack_shape, shape((sec, 1, 128), F32)],
        [core_id, got, precond],
        smem=1,
    )
    h_chip, h_core = far(outer), near(inner)
    packs = [h_core, h_chip]
    row = exchange(row, "sec")
    dir_all, m_dir, coef = call(
        form_kernel,
        [four_shape, four_shape, shape((6, 8, 128), F32)],
        [row, got, h_core, h_chip, start_all, precond, *packs],
    )
    parts, dir_all, m_dir = barrier((apply_op(dir_all), dir_all, m_dir))
    got = exchange(parts)
    h_dir, body = call(
        functools.partial(settle_kernel, factor),
        [slice_shape, shape((groups, lines, states), BF)],
        [got, mask_rows],
    )
    got = exchange(body)
    got, h_dir, m_dir, start_all = barrier((got, h_dir, m_dir, start_all))
    inner, outer = call(unpack_kernel, [edge_shape, edge_shape], [core_id, got], smem=1)
    hd_chip, hd_core = far(outer), near(inner)
    (m_start,) = call(lift_start_kernel, [four_shape], [start_all, precond, *packs])
    known = [m_start, m_dir, dir_all, start_all]
    h_m_start, dots_start = apply_op(m_start, known)
    h_m_dir, dots_dir = apply_op(m_dir, known)
    gram, direction = call(
        gram_kernel,
        [shape((len(PLAIN) + 2 * len(PAIRS), vecs, 8, 128), F32), slice_shape],
        [coef, vec, h_raw, h_dir, pre],
    )
    (m_hd,) = call(lift_kernel, [four_shape], [got, hd_core, hd_chip, precond, *packs])
    dots_hd = apply_op(m_hd, [m_hd] + known, [h_m_start, h_m_dir], keep=False)
    everyone = groups * sec
    (row,) = call(
        functools.partial(tally_kernel, factor),
        [shape((everyone, 1, 128), F32)],
        [gram, dots_hd, dots_start, dots_dir],
    )
    row = exchange(row, ("term", "sec"))
    final, energy = call(
        finish_kernel,
        [slice_shape, shape((vecs,), F32)],
        [row, coef, vec, direction, h_raw, h_dir, pre],
        smem_outs=1,
    )
    return (final, energy)


def solution(mesh):
    return jax.shard_map(
        shards,
        mesh=mesh,
        in_specs=(
            P(None, "sec", None, None),
            P("term", "sec", None, None),
            P("term", "sec", None, None),
            P("term"),
            P("sec", None, None),
            P("sec"),
        ),
        out_specs=(P(None, "sec", "term", None), P()),
        check_vma=False,
    )
```

```python
import functools

import jax
import jax.numpy as jnp
from jax import lax
from jax.experimental import pallas as pl
from jax.experimental.pallas import tpu as pltpu
from jax.sharding import PartitionSpec as P


BF = jnp.bfloat16
F32 = jnp.float32
PAIRS = [(i, j) for i in range(4) for j in range(i, 4)]
PLAIN = [(0, 0), (0, 1), (1, 1), (0, 2), (0, 3), (1, 2), (1, 3)]
EXTRA = 16


def fold(product):
    rows, cols = product.shape
    tile = jnp.sum(product.reshape(rows // 8, 8, cols), axis=0)
    return sum(tile[:, i : i + 128] for i in range(0, cols, 128))


def slot_of(core_ref, shift_ref, k, b):
    at, core = b + shift_ref[k], core_ref[0]
    return jnp.where(at < 0, 3 - core, jnp.where(at > 1, 2 + core, at))


def apply_kernel(count, core_ref, shift_ref, x_ref, right_ref, left_ref, *refs):
    field_refs, paired_refs, rest = refs[: count[0]], refs[count[0] : sum(count)], refs[sum(count) :]
    out_ref, z_ref = rest[0], rest[-1]
    vecs, _, states, _ = x_ref.shape
    terms, blocks = left_ref.shape[:2]
    for k in range(terms):
        for b in range(blocks):
            slot = slot_of(core_ref, shift_ref, k, b)
            x = x_ref[:, slot].reshape(vecs * states, states)
            z = lax.dot_general(
                x, right_ref[k, slot], (((1,), (1,)), ((), ())), preferred_element_type=F32
            ).astype(BF)
            for u in range(vecs):
                z_ref[b, pl.ds(k * states, states), pl.ds(u * states, states)] = z[
                    u * states : (u + 1) * states
                ]
    if sum(count):
        dot_ref = rest[-2]
        dot_ref[...] = jnp.zeros_like(dot_ref)
    for b in range(blocks):
        wide = jnp.concatenate([left_ref[k, b] for k in range(terms)], axis=1)
        acc = jnp.dot(wide, z_ref[b], preferred_element_type=F32)
        for u in range(vecs):
            part = acc[:, u * states : (u + 1) * states]
            if not sum(count):
                groups, share = out_ref.shape[0], out_ref.shape[3]
                out_ref[:, u, b] = part.reshape(groups, share, states).astype(out_ref.dtype)
            elif len(rest) == 3:
                out_ref[u, b] = part.astype(out_ref.dtype)
            products = [part * f[u, b].astype(F32) for f in field_refs]
            products += [x_ref[u, b].astype(F32) * f[u, b].astype(F32) for f in paired_refs]
            for i, product in enumerate(products):
                dot_ref[i, u] = dot_ref[i, u] + fold(product)


def settle_kernel(factor, got_ref, mask_ref, *refs):
    h_ref, body_ref = refs[-2:]
    groups, vecs, blocks, share, states = got_ref.shape
    row = jnp.zeros((1, 128), F32)
    lane = lax.broadcasted_iota(jnp.int32, (1, 128), 1)
    for u in range(vecs):
        tiles = [jnp.zeros((8, 128), F32) for _ in range(8)]
        for b in range(blocks):
            h = got_ref[0, u, b].astype(F32)
            for t in range(1, groups):
                h = h + got_ref[t, u, b].astype(F32)
            h = h * mask_ref[b]
            h_ref[u, b] = h
            small = h.astype(BF)
            for t in range(groups):
                body_ref[t, pl.ds((u * blocks + b) * share, share), :] = small
            if len(refs) == 4:
                v, m = refs[0][u, b].astype(F32), refs[1][b]
                mv, mh = m * v, m * h
                products = [v * v, v * h, v * mv, v * mh, h * mh, mv * mv, mv * mh, mh * mh]
                tiles = [x + fold(y) for x, y in zip(tiles, products)]
        if len(refs) == 4:
            for i, tile in enumerate(tiles):
                row = row + jnp.where(lane == i * vecs + u, jnp.sum(tile) * factor, 0.0)
    if len(refs) == 4:
        high = row.astype(BF).astype(F32)
        middle = (row - high).astype(BF).astype(F32)
        low = row - high - middle
        index = lax.broadcasted_iota(jnp.int32, (EXTRA, 128), 0)
        tile = jnp.where(index == 0, high, jnp.where(index == 1, middle, jnp.where(index == 2, low, 0.0)))
        tile = tile.astype(BF)
        for t in range(groups):
            body_ref[t, pl.ds(vecs * blocks * share, EXTRA), pl.ds(0, 128)] = tile
            body_ref[t, pl.ds(vecs * blocks * share, EXTRA), pl.ds(128, states - 128)] = jnp.zeros(
                (EXTRA, states - 128), BF
            )


def block_of(got_ref, u, b, blocks, share):
    groups, _, states = got_ref.shape
    start = (u * blocks + b) * share
    if not isinstance(start, int):
        start = pl.multiple_of(start, share)
    return got_ref[:, pl.ds(start, share), :].reshape(groups * share, states)


def unpack_kernel(core_ref, got_ref, *refs):
    inner_ref, outer_ref = refs[1:3] if len(refs) == 4 else refs
    groups, _, states = got_ref.shape
    vecs, share = 2, states // groups
    core = core_ref[0]
    for ref, b in ((inner_ref, 1 - core), (outer_ref, core)):
        for u in range(vecs):
            ref[u] = block_of(got_ref, u, b, 2, share)
        if len(refs) == 4:
            ref[vecs] = refs[0][b].astype(BF)
    if len(refs) == 4:
        tile = jnp.zeros((EXTRA, 128), F32)
        for t in range(groups):
            tile = tile + got_ref[t, pl.ds(vecs * 2 * share, EXTRA), pl.ds(0, 128)].astype(F32)
        row_ref = refs[3]
        row_ref[...] = jnp.broadcast_to(jnp.sum(tile, axis=0, keepdims=True)[None], row_ref.shape)


def slot_blocks(own_ref, core_ref, chip_ref, u, share):
    own = [block_of(own_ref, u, b, 2, share) for b in range(2)]
    return own + [core_ref[u], chip_ref[u]]


def pick(row, i, vecs):
    return row if i == 0 else pltpu.roll(row, 128 - i * vecs, 1)


def lane_of(row, u):
    lane = lax.broadcasted_iota(jnp.int32, row.shape, 1)
    return jnp.sum(jnp.where(lane == u, row, 0.0), axis=1, keepdims=True)


def weight_of(own_ref, core_ref, chip_ref, i):
    if i < 2:
        return own_ref[i]
    ref = (core_ref, chip_ref)[i - 2]
    return ref[ref.shape[0] - 1].astype(F32)


def form_kernel(row_ref, got_ref, core_ref, chip_ref, start_ref, pre_ref, pre_core, pre_chip, dir_ref, coef_ref):
    vecs, slots, states, _ = dir_ref.shape
    share = states // got_ref.shape[0]
    row = row_ref[0]
    for i in range(1, row_ref.shape[0]):
        row = row + row_ref[i]
    total = [pick(row, i, vecs) for i in range(8)]
    scale = 1.0 / jnp.sqrt(total[0] + 1e-06)
    vv, vh, vmv, vmh, hmh, mvmv, mvmh, mhmh = [x * (scale * scale) for x in total]
    correlation = vmh - vh * vmv
    square = mhmh - 2.0 * vh * mvmh + vh * vh * mvmv
    square = square - 2.0 * correlation * (vmh - vh * vmv) + correlation * correlation * vv
    norm = jnp.sqrt(jnp.maximum(square, 0.0) + 1e-06)
    coupling = (hmh - vh * vmh - correlation * vh) / norm
    alpha = scale / norm
    for j, x in enumerate([vh, correlation, alpha, scale, coupling, norm]):
        coef_ref[j] = jnp.broadcast_to(x, coef_ref.shape[1:])
    for u in range(vecs):
        ray, corr, mult = [lane_of(x[0:1], u) for x in (vh, correlation, alpha)]
        hs = slot_blocks(got_ref, core_ref, chip_ref, u, share)
        for i in range(slots):
            m = weight_of(pre_ref, pre_core, pre_chip, i)
            v = start_ref[u, i].astype(F32)
            raw = m * (hs[i].astype(F32) - ray * v) - corr * v
            dir_ref[u, i] = (raw * mult).astype(BF)


def lift_kernel(got_ref, core_ref, chip_ref, pre_ref, pre_core, pre_chip, out_ref):
    vecs, slots, states, _ = out_ref.shape
    share = states // got_ref.shape[0]
    for u in range(vecs):
        hs = slot_blocks(got_ref, core_ref, chip_ref, u, share)
        for i in range(slots):
            m = weight_of(pre_ref, pre_core, pre_chip, i)
            out_ref[u, i] = (m * hs[i].astype(F32)).astype(BF)


def lift_start_kernel(start_ref, pre_ref, pre_core, pre_chip, out_ref):
    vecs, slots = out_ref.shape[:2]
    for u in range(vecs):
        for i in range(slots):
            m = weight_of(pre_ref, pre_core, pre_chip, i)
            out_ref[u, i] = (m * start_ref[u, i].astype(F32)).astype(BF)


def gram_kernel(coef_ref, start_ref, h_ref, hd_ref, pre_ref, dot_ref, dir_ref):
    vecs, blocks = h_ref.shape[:2]
    for u in range(vecs):
        rayleigh, correlation, alpha, scale = [lane_of(coef_ref[j, 0:1], u) for j in range(4)]
        for b in range(blocks):
            m = pre_ref[b]
            v, h = start_ref[u, b].astype(F32), h_ref[u, b]
            d = (m * (h - rayleigh * v) - correlation * v) * alpha
            dir_ref[u, b] = d
            basis = [v * scale, d, h * scale, hd_ref[u, b]]
            lifted = [m * x for x in basis]
            products = [basis[i] * basis[j] for i, j in PLAIN]
            products += [basis[i] * lifted[j] for i, j in PAIRS]
            products += [lifted[i] * lifted[j] for i, j in PAIRS]
            for i, product in enumerate(products):
                tile = fold(product)
                dot_ref[i, u] = tile if b == 0 else dot_ref[i, u] + tile


def tally_kernel(factor, *refs):
    out_ref = refs[-1]
    lines = []
    for ref in refs[:-1]:
        for i in range(ref.shape[0]):
            lines += [jnp.sum(ref[i, u], axis=0, keepdims=True) for u in range(ref.shape[1])]
    lines.append(jnp.zeros((128 - len(lines), 128), F32))
    table = jnp.concatenate(lines, axis=0)
    row = lax.dot_general(
        jnp.ones((8, 128), F32),
        table,
        (((1,), (1,)), ((), ())),
        precision=lax.Precision.HIGHEST,
        preferred_element_type=F32,
    )
    out_ref[...] = jnp.broadcast_to((row[0:1] * factor)[None], out_ref.shape)


def pack_kernel(core_ref, dims_hbm, start_ref, right_ref, out_ref, dims_ref, raw, sem):
    terms, vecs = right_ref.shape[0], start_ref.shape[0]
    states = out_ref.shape[1]
    b = core_ref[0]
    copies = [pltpu.make_async_copy(dims_hbm, dims_ref, sem.at[0])]
    copies += [pltpu.make_async_copy(start_ref.at[u, b], raw.at[u], sem.at[1 + u]) for u in range(vecs)]
    for k in range(terms):
        copies.append(pltpu.make_async_copy(right_ref.at[k, b], out_ref.at[k], sem.at[1 + vecs + k]))
    for copy in copies:
        copy.start()
    for copy in copies[: vecs + 1]:
        copy.wait()
    row = lax.broadcasted_iota(jnp.int32, (states, states), 0)
    col = lax.broadcasted_iota(jnp.int32, (states, states), 1)
    keep = (row < dims_ref[b]) & (col < dims_ref[b])
    for u in range(vecs):
        out_ref[terms + u] = jnp.where(keep, raw[u].astype(F32), 0.0).astype(BF)
    for copy in copies[vecs + 1 :]:
        copy.wait()


def load_kernel(core_ref, term_ref, dims_ref, shift_ref, start_ref, left_ref, right_ref, pre_ref, own_ref, left_out, right_out, mask_out, pre_out, vec_out, near_out, raw, weights, sem):
    vecs, blocks, states, _ = own_ref.shape
    terms = left_ref.shape[0]
    share = vec_out.shape[2]
    core = core_ref[0]
    first = pltpu.make_async_copy(start_ref, raw, sem.at[0])
    second = pltpu.make_async_copy(pre_ref, weights, sem.at[1])
    rest = []
    for k in range(terms):
        rest.append(pltpu.make_async_copy(right_ref.at[k, 1 - core], near_out.at[k], sem.at[2 + 3 * k]))
        rest.append(pltpu.make_async_copy(right_ref.at[k], right_out.at[k], sem.at[3 + 3 * k]))
        rest.append(pltpu.make_async_copy(left_ref.at[k], left_out.at[k], sem.at[4 + 3 * k]))
    for copy in [first, second] + rest:
        copy.start()
    here = pl.ds(pl.multiple_of(term_ref[0] * share, share), share)
    row = lax.broadcasted_iota(jnp.int32, (states, states), 0)
    col = lax.broadcasted_iota(jnp.int32, (states, states), 1)
    first.wait()
    for b in range(blocks):
        keep = (row < dims_ref[b]) & (col < dims_ref[b])
        for u in range(vecs):
            own_ref[u, b] = jnp.where(keep, raw[u, b].astype(F32), 0.0).astype(BF)
            vec_out[u, b] = own_ref[u, b, here, :]
        low = row[:share] + term_ref[0] * share
        mask_out[b] = jnp.where((low < dims_ref[b]) & (col[:share] < dims_ref[b]), 1.0, 0.0)
    second.wait()
    for b in range(blocks):
        pre_out[b] = weights[b, here, :]
    for u in range(vecs):
        near_out[terms + u] = own_ref[u, 1 - core]
    for copy in rest:
        copy.wait()


def form(table, left, right):
    result = None
    for i, x in left:
        for j, y in right:
            term = x * y * table[(min(i, j), max(i, j))]
            result = term if result is None else result + term
    return result


def lowest(rayleigh, curvature, coupling):
    half = 0.5 * (rayleigh - curvature)
    energy = 0.5 * (rayleigh + curvature) - jnp.sqrt(half * half + coupling * coupling)
    weight = energy - rayleigh
    return energy, weight, jnp.sqrt(coupling * coupling + weight * weight)


def finish_kernel(row_ref, coef_ref, start_ref, dir_ref, h_ref, hd_ref, pre_ref, out_ref, energy_ref):
    vecs, blocks = out_ref.shape[:2]
    chains = [row_ref[i] for i in range(16)]
    for i in range(16, row_ref.shape[0]):
        chains[i % 16] = chains[i % 16] + row_ref[i]
    while len(chains) > 1:
        chains = [x + y for x, y in zip(chains[::2], chains[1::2])]
    row = chains[0]
    count = len(PLAIN) + 2 * len(PAIRS) + 15
    total = [pick(row, i, vecs) for i in range(count)]
    one = {p: total[i] for i, p in enumerate(PLAIN)}
    first = {p: total[len(PLAIN) + i] for i, p in enumerate(PAIRS)}
    second = {p: total[len(PLAIN) + len(PAIRS) + i] for i, p in enumerate(PAIRS)}
    far = total[len(PLAIN) + 2 * len(PAIRS) :]
    old_ray, old_corr, _, scale, coupling, old_norm = [coef_ref[j, 0:1] for j in range(6)]

    _, weight, size = lowest(old_ray, one[(1, 3)], coupling)
    keep, mix = coupling / size, weight / size
    v_of, h_of = [(0, keep), (1, mix)], [(2, keep), (3, mix)]
    rayleigh = form(one, v_of, h_of)
    resid_of = h_of + [(i, -rayleigh * x) for i, x in v_of]
    correlation = form(first, v_of, resid_of)
    square = form(second, resid_of, resid_of) - 2.0 * correlation * form(first, v_of, resid_of)
    square = square + correlation * correlation * form(one, v_of, v_of)
    norm = jnp.sqrt(jnp.maximum(square, 0.0) + 1e-06)
    coupling = (form(first, resid_of, h_of) - correlation * rayleigh) / norm

    mult = [
        mix,
        scale * keep * (old_ray - rayleigh),
        -rayleigh * mix,
        keep * old_norm - correlation * mix,
        scale * keep * (old_corr - correlation),
    ]
    back = 1.0 / scale
    on_hd = far[:5]
    on_start = [far[5]] + [far[7 + i] for i in range(4)]
    on_dir = [far[6]] + [far[11 + i] for i in range(4)]
    on_d = [first[3, 3], first[0, 3] * back, first[1, 3], one[1, 3], one[0, 3] * back]
    on_v = [first[2, 3], first[0, 2] * back, first[1, 2], one[1, 2], one[0, 2] * back]
    curvature = None
    for j, column in enumerate([on_hd, on_start, on_dir, on_d, on_v]):
        line = None
        for i in range(5):
            term = mult[i] * column[i]
            line = term if line is None else line + term
        line = line * (mult[j] * back if j == 4 else mult[j])
        curvature = line if curvature is None else curvature + line
    curvature = curvature / (norm * norm)
    energy, weight, size = lowest(rayleigh, curvature, coupling)
    of_v, of_raw = coupling / size, weight / (norm * size)
    values = (keep * scale, mix, rayleigh, correlation, of_v, of_raw)
    for u in range(vecs):
        energy_ref[u] = lane_of(energy, u)[0, 0]
        first_v, then_d, ray, corr, use_v, use_raw = [lane_of(x, u) for x in values]
        for b in range(blocks):
            new_v = first_v * start_ref[u, b].astype(F32) + then_d * dir_ref[u, b]
            new_h = first_v * h_ref[u, b] + then_d * hd_ref[u, b]
            raw = pre_ref[b] * (new_h - ray * new_v) - corr * new_v
            out_ref[u, b] = use_v * new_v + use_raw * raw


def call(kernel, outs, args, smem=0, scratch=(), flops=0, smem_outs=0, anywhere=False):
    vmem = pl.BlockSpec(memory_space=pltpu.VMEM)
    bulk = pl.BlockSpec(memory_space=pltpu.HBM) if anywhere else vmem
    specs = [pl.BlockSpec(memory_space=pltpu.SMEM)] * smem + [bulk] * (len(args) - smem)
    size = sum(x.size * x.dtype.itemsize for x in list(outs) + list(args))
    return pl.pallas_call(
        kernel,
        out_shape=[jax.ShapeDtypeStruct(x.shape, x.dtype) for x in outs],
        in_specs=specs,
        out_specs=[vmem] * (len(outs) - smem_outs)
        + [pl.BlockSpec(memory_space=pltpu.SMEM)] * smem_outs,
        scratch_shapes=scratch,
        compiler_params=pltpu.CompilerParams(vmem_limit_bytes=24 << 20),
        cost_estimate=pl.CostEstimate(flops=flops, bytes_accessed=size, transcendentals=0),
    )(*args)


def shards(start_vectors, left_env, right_env, term_shift, precond, block_dims):
    vecs, blocks, states, _ = start_vectors.shape
    groups = lax.axis_size("term")
    sec = lax.axis_size("sec")
    share = states // groups
    core_id = (lax.axis_index("sec") & 1).reshape(1)
    term_id = lax.axis_index("term").reshape(1)
    factor = 1.0 / (blocks * sec * states * states)
    shape = jax.ShapeDtypeStruct

    core_pairs = [(i, i ^ 1) for i in range(sec)]
    chip_pairs = [(i, i + 1) for i in range(1, sec - 1, 2)]
    chip_pairs = chip_pairs + [(j, i) for i, j in chip_pairs]

    def far(x):
        return lax.ppermute(x, "sec", chip_pairs)

    def near(x):
        return lax.ppermute(x, "sec", core_pairs)

    def apply_op(x, fields=(), paired=(), keep=True):
        outs = []
        if not fields:
            outs = [shape((groups, vecs, blocks, share, states), BF)]
        elif keep:
            outs = [shape((vecs, blocks, states, states), BF)]
        count = (len(fields), len(paired))
        if sum(count):
            outs.append(shape((sum(count), vecs, 8, 128), F32))
        result = call(
            functools.partial(apply_kernel, count),
            outs,
            [core_id, term_shift, x, right_all, left_here, *fields, *paired],
            smem=2,
            scratch=[pltpu.VMEM((blocks, left_env.shape[0] * states, vecs * states), BF)],
            flops=16 * vecs * blocks * states**3,
        )
        return result[0] if len(outs) == 1 else result

    def exchange(parts, axis="term"):
        return lax.all_to_all(parts, axis, 0, 0)

    barrier = lax.optimization_barrier

    slice_shape = shape((vecs, blocks, share, states), F32)
    edge_shape = shape((vecs, states, states), BF)
    four_shape = shape((vecs, 4, states, states), BF)
    lines = vecs * blocks * share
    terms = right_env.shape[0]

    def in_hbm(x):
        return pltpu.with_memory_space_constraint(x, pltpu.HBM)

    start_hbm, left_hbm, right_hbm, pre_hbm = [
        in_hbm(x) for x in (start_vectors, left_env, right_env, precond)
    ]

    (pack_chip,) = call(
        pack_kernel,
        [shape((terms + vecs, states, states), BF)],
        [core_id, in_hbm(block_dims), start_hbm, right_hbm],
        smem=1,
        scratch=[
            pltpu.SMEM(block_dims.shape, jnp.int32),
            pltpu.VMEM((vecs, states, states), BF),
            pltpu.SemaphoreType.DMA((1 + vecs + terms,)),
        ],
        anywhere=True,
    )
    pack_chip = far(pack_chip)
    start, left_here, right_here, mask_rows, pre, vec, pack_core = call(
        load_kernel,
        [
            shape(start_vectors.shape, BF),
            shape(left_env.shape, BF),
            shape(right_env.shape, BF),
            shape((blocks, share, states), F32),
            shape((blocks, share, states), F32),
            shape((vecs, blocks, share, states), BF),
            shape((terms + vecs, states, states), BF),
        ],
        [core_id, term_id, block_dims, term_shift, start_hbm, left_hbm, right_hbm, pre_hbm],
        smem=4,
        scratch=[
            pltpu.VMEM(start_vectors.shape, BF),
            pltpu.VMEM(precond.shape, F32),
            pltpu.SemaphoreType.DMA((2 + 3 * terms,)),
        ],
        anywhere=True,
    )
    pack_core = near(pack_core)
    packs = [pack_core, pack_chip]
    right_all = jnp.concatenate([right_here] + [x[:terms, None] for x in packs], axis=1)
    start_all = jnp.concatenate([start] + [x[terms:, None] for x in packs], axis=1)
    got = exchange(apply_op(start_all))
    h_raw, body = call(
        functools.partial(settle_kernel, factor),
        [slice_shape, shape((groups, lines + EXTRA, states), BF)],
        [got, mask_rows, vec, pre],
    )
    got = exchange(body)
    pack_shape = shape((vecs + 1, states, states), BF)
    inner, outer, row = call(
        unpack_kernel,
        [pack_shape, pack_shape, shape((sec, 1, 128), F32)],
        [core_id, got, precond],
        smem=1,
    )
    h_chip, h_core = far(outer), near(inner)
    packs = [h_core, h_chip]
    row = exchange(row, "sec")
    dir_all, coef = call(
        form_kernel,
        [four_shape, shape((6, 8, 128), F32)],
        [row, got, h_core, h_chip, start_all, precond, *packs],
    )
    parts, dir_all = barrier((apply_op(dir_all), dir_all))
    got = exchange(parts)
    h_dir, body = call(
        functools.partial(settle_kernel, factor),
        [slice_shape, shape((groups, lines, states), BF)],
        [got, mask_rows],
    )
    got = exchange(body)
    got, h_dir, dir_all, start_all = barrier((got, h_dir, dir_all, start_all))
    inner, outer = call(unpack_kernel, [edge_shape, edge_shape], [core_id, got], smem=1)
    hd_chip, hd_core = far(outer), near(inner)
    (m_start,) = call(lift_start_kernel, [four_shape], [start_all, precond, *packs])
    (m_dir,) = call(lift_start_kernel, [four_shape], [dir_all, precond, *packs])
    known = [m_start, m_dir, dir_all, start_all]
    h_m_start, dots_start = apply_op(m_start, known)
    h_m_dir, dots_dir = apply_op(m_dir, known)
    gram, direction = call(
        gram_kernel,
        [shape((len(PLAIN) + 2 * len(PAIRS), vecs, 8, 128), F32), slice_shape],
        [coef, vec, h_raw, h_dir, pre],
    )
    (m_hd,) = call(lift_kernel, [four_shape], [got, hd_core, hd_chip, precond, *packs])
    dots_hd = apply_op(m_hd, [m_hd] + known, [h_m_start, h_m_dir], keep=False)
    everyone = groups * sec
    (row,) = call(
        functools.partial(tally_kernel, factor),
        [shape((everyone, 1, 128), F32)],
        [gram, dots_hd, dots_start, dots_dir],
    )
    row = exchange(row, ("term", "sec"))
    final, energy = call(
        finish_kernel,
        [slice_shape, shape((vecs,), F32)],
        [row, coef, vec, direction, h_raw, h_dir, pre],
        smem_outs=1,
    )
    return (final, energy)


def solution(mesh):
    return jax.shard_map(
        shards,
        mesh=mesh,
        in_specs=(
            P(None, "sec", None, None),
            P("term", "sec", None, None),
            P("term", "sec", None, None),
            P("term"),
            P("sec", None, None),
            P("sec"),
        ),
        out_specs=(P(None, "sec", "term", None), P()),
        check_vma=False,
    )
```
